32 devices in a mesh: section: 2 (over x), render: 2 (over core), dp: 8 (over z, y).
Axes of the slice: x: 2, y: 2, z: 4, core: 2. Of those that a mesh axis runs over, the one named last changes fastest.
Arguments:
- section_tokens: bfloat16 [2, 8, 256, 2048], P('section', 'dp', 'render'), may hold values from -60 to 60
- w_qkv: bfloat16 [2, 2048, 3072], P('section', 'dp'), may hold values from -0.5 to 0.5
- w_out: bfloat16 [2, 1024, 2048], P('section', 'dp'), may hold values from -0.1875 to 0.1875
- gains: float32 [2, 2048], P('section'), may hold values from 0.25 to 1.75
- cotangent: bfloat16 [8, 256, 2048], P('dp', 'render'), may hold values from -6 to 6
Outputs:
- token_grads: bfloat16 [2, 8, 256, 2048], P('section', 'dp', 'render')
- qkv_grads: float32 [2, 2048, 3072], P('section', 'dp')
- out_grads: float32 [2, 1024, 2048], P('section', 'dp')
- gain_grads: float32 [2, 2048], P('section')
The draws below stay inside these ranges and needn't reach their ends.
All inputs are finite; a program needn't handle non-finite values.
Results may differ from the reference program's by a relative error of at most 0.02.
Values may be sent and summed in bfloat16 or wider, within the bound.
A program may use at most 192 MiB of HBM per device.

```python
import math
import jax
import jax.numpy as jnp
from jax import lax

D = 2048
HEADS = 8
HD = 128
ROWS = 128
HW = 1024
TOKS = 256
SCENES = 8
N_RENDER = 2


def draw_section_tokens(key, part):
    full_shape = (2, SCENES, TOKS, D)
    base_noise = jax.random.normal(jax.random.fold_in(key, 1), full_shape, jnp.float32)
    tokens = base_noise
    return jnp.clip(tokens, -60.0, 60.0).astype(jnp.bfloat16)


def draw_w_qkv(key, part):
    full_shape = (2, D, 3 * HEADS * HD)
    weight = jnp.clip(jax.random.normal(jax.random.fold_in(key, 5), full_shape, jnp.float32), -6.0, 6.0) / math.sqrt(D)
    return jnp.clip(weight, -0.5, 0.5).astype(jnp.bfloat16)


def level_of(stream_key, dims, cuts, low, largest):
    loudness = 1.0
    for dim, blocks in cuts:
        steps = jax.random.uniform(jax.random.fold_in(jax.random.fold_in(stream_key, 6), dim), (blocks,), jnp.float32, low / len(cuts), largest / len(cuts))
        loudness = loudness * jnp.repeat(jnp.exp(steps), dims[dim] // blocks).reshape((-1,) + (1,) * (len(dims) - 1 - dim))
    return loudness


def gaussian(own_key, extent, width, bound, split=(), dtype=jnp.bfloat16):
    entries = jax.random.normal(own_key, extent, jnp.float32) * width
    if len(split) > 0:
        entries = level_of(own_key, extent, split, -0.22, 0.18) * entries
    return jnp.clip(entries, min=-bound, max=bound).astype(dtype)


def setup_inputs(seed: int = 0) -> dict:
    key_of = jax.random.split(jax.random.key(seed), 6)
    section_tokens = draw_section_tokens(jax.random.fold_in(key_of[5], 71), 0)
    w_qkv = draw_w_qkv(jax.random.fold_in(key_of[5], 71), 0)
    w_out = gaussian(key_of[2], (2, HW, D), HW ** -0.5, 0.1875, ((0, 2), (1, 8)))
    gains = jnp.clip(1.0 + 0.15 * jax.random.normal(key_of[3], (2, D), jnp.float32), 0.25, 1.75)
    cotangent = gaussian(key_of[4], (SCENES, TOKS, D), 1.0, 6.0, ((0, 8), (1, 2)))
    return {"section_tokens": section_tokens, "w_qkv": w_qkv, "w_out": w_out, "gains": gains, "cotangent": cotangent}


NORM_EPSILON = 1e-06

def rms_norm(values, gain_row):
    wide_rows = values.astype(jnp.float32)
    row_scale = lax.rsqrt(lax.optimization_barrier(jnp.mean(wide_rows * wide_rows, axis=-1, keepdims=True)) + NORM_EPSILON)
    return ((wide_rows * row_scale * gain_row).astype(jnp.bfloat16), row_scale)

def norm_back(values, row_scale, gain_row, upstream):
    wide_rows = values.astype(jnp.float32)
    grad_wide = upstream.astype(jnp.float32)
    scaled = grad_wide * gain_row
    inner_sum = lax.optimization_barrier(jnp.sum(scaled * wide_rows, axis=-1, keepdims=True))
    result = row_scale * scaled - wide_rows * row_scale ** 3 * inner_sum / values.shape[-1]
    gain_term = lax.optimization_barrier(jnp.sum(grad_wide * wide_rows * row_scale, axis=0))
    return (result, gain_term)

def to_half(values):
    return lax.optimization_barrier(values.astype(jnp.bfloat16)).astype(jnp.float32)

def matmul(left, right):
    return jnp.dot(left, right, preferred_element_type=jnp.float32)

def split_heads(values):
    return values.astype(jnp.float32).reshape(values.shape[0], HEADS, HD)

def attend(queries, key_rows, value_rows):
    factor = HD ** (-0.5)
    scores = jnp.einsum('qhd,khd->hqk', split_heads(queries), split_heads(key_rows)) * factor
    row_top = lax.optimization_barrier(jnp.max(scores, axis=-1, keepdims=True))
    raised = jnp.exp(scores - row_top)
    row_total = lax.optimization_barrier(jnp.sum(raised, axis=-1, keepdims=True))
    attn_prob = raised / row_total
    mixed_heads = jnp.einsum('hqk,khd->qhd', to_half(attn_prob), split_heads(value_rows))
    return (mixed_heads.reshape(queries.shape[0], HEADS * HD).astype(jnp.bfloat16), attn_prob)

def attend_back(queries, key_rows, value_rows, attn_prob, upstream):
    factor = HD ** (-0.5)
    grad_prob = jnp.einsum('qhd,khd->hqk', split_heads(upstream), split_heads(value_rows))
    row_delta = lax.optimization_barrier(jnp.sum(grad_prob * attn_prob, axis=-1, keepdims=True))
    grad_score = to_half(attn_prob * (grad_prob - row_delta) * factor)
    grad_query = jnp.einsum('hqk,khd->qhd', grad_score, split_heads(key_rows)).reshape(queries.shape[0], HEADS * HD)
    grad_key = jnp.einsum('hqk,qhd->khd', grad_score, split_heads(queries)).reshape(key_rows.shape[0], HEADS * HD)
    grad_value = jnp.einsum('hqk,qhd->khd', to_half(attn_prob), split_heads(upstream)).reshape(key_rows.shape[0], HEADS * HD)
    return (grad_query, grad_key, grad_value)

def reference(section_tokens, w_qkv, w_out, gains, cotangent):
    head_width = HEADS * HD
    half_rows = ROWS // 2
    lat_rows = N_RENDER * half_rows
    scene_rows = N_RENDER * ROWS
    enc_qkv = w_qkv[0]
    dec_qkv = w_qkv[1]
    enc_out = w_out[0]
    dec_out = w_out[1]
    enc_gain = gains[0].astype(jnp.float32)
    dec_gain = gains[1].astype(jnp.float32)

    def scene_step(totals, inputs):
        enc_tokens, dec_tokens, upstream = inputs
        enc_norm, enc_scale = rms_norm(enc_tokens, enc_gain)
        enc_proj = matmul(enc_norm, enc_qkv).astype(jnp.bfloat16)
        blocked = enc_proj.reshape(N_RENDER, ROWS, 3 * head_width)
        lat_query = blocked[:, half_rows:, :head_width].reshape(lat_rows, head_width)
        lat_input = enc_tokens.reshape(N_RENDER, ROWS, D)[:, half_rows:].reshape(lat_rows, D)
        lat_norm_enc = enc_norm.reshape(N_RENDER, ROWS, D)[:, half_rows:].reshape(lat_rows, D)
        enc_keys = enc_proj[:, head_width:2 * head_width]
        enc_values = enc_proj[:, 2 * head_width:]
        enc_mixed, enc_prob = attend(lat_query, enc_keys, enc_values)
        latent = (lat_input.astype(jnp.float32) + matmul(enc_mixed, enc_out)).astype(jnp.bfloat16)
        lat_norm, lat_scale = rms_norm(latent, dec_gain)
        lat_kv = matmul(lat_norm, dec_qkv[:, head_width:]).astype(jnp.bfloat16)
        dec_norm, dec_scale = rms_norm(dec_tokens, dec_gain)
        dec_proj = matmul(dec_norm, dec_qkv).astype(jnp.bfloat16)
        lat_grad_sum = jnp.zeros((lat_rows, 2 * head_width), jnp.float32)
        dec_out_sum = jnp.zeros((head_width, D), jnp.float32)
        view_grads = []
        for view_index in range(N_RENDER):
            first = view_index * ROWS
            proj_view = dec_proj[first:first + ROWS]
            key_rows = jnp.concatenate([lat_kv[:, :head_width], proj_view[:, head_width:2 * head_width]], 0)
            value_rows = jnp.concatenate([lat_kv[:, head_width:], proj_view[:, 2 * head_width:]], 0)
            mixed_view, prob_view = attend(proj_view[:, :head_width], key_rows, value_rows)
            cot_view = upstream[first:first + ROWS]
            dec_out_sum = dec_out_sum + to_half(matmul(mixed_view.T, cot_view))
            grad_mixed = matmul(cot_view, dec_out.T).astype(jnp.bfloat16)
            grad_query, grad_key, grad_value = attend_back(proj_view[:, :head_width], key_rows, value_rows, prob_view, grad_mixed)
            lat_grad_sum = lat_grad_sum + jnp.concatenate([grad_key[:lat_rows], grad_value[:lat_rows]], 1)
            view_grads.append(jnp.concatenate([grad_query, grad_key[lat_rows:], grad_value[lat_rows:]], 1).astype(jnp.bfloat16))
        lat_grad = lat_grad_sum.astype(jnp.bfloat16)
        dec_grad_proj = jnp.concatenate(view_grads, 0)
        dec_qkv_sum = jnp.zeros((D, 3 * head_width), jnp.float32)
        for view_index in range(N_RENDER):
            first = view_index * ROWS
            lat_first = view_index * half_rows
            partial_sum = matmul(dec_norm[first:first + ROWS].T, dec_grad_proj[first:first + ROWS])
            extra_sum = matmul(lat_norm[lat_first:lat_first + half_rows].T, lat_grad[lat_first:lat_first + half_rows])
            partial_sum = partial_sum.at[:, head_width:].add(extra_sum)
            dec_qkv_sum = dec_qkv_sum + to_half(partial_sum)
        grad_dec_norm = matmul(dec_grad_proj, dec_qkv.T).astype(jnp.bfloat16)
        grad_lat_norm = matmul(lat_grad, dec_qkv[:, head_width:].T).astype(jnp.bfloat16)
        dec_back, dec_gain_first = norm_back(dec_tokens, dec_scale, dec_gain, grad_dec_norm)
        dec_result = (upstream.astype(jnp.float32) + dec_back).astype(jnp.bfloat16)
        lat_back, dec_gain_second = norm_back(latent, lat_scale, dec_gain, grad_lat_norm)
        lat_upstream = lat_back.astype(jnp.bfloat16)
        grad_enc_mixed = matmul(lat_upstream, enc_out.T).astype(jnp.bfloat16)
        grad_query, grad_key, grad_value = attend_back(lat_query, enc_keys, enc_values, enc_prob, grad_enc_mixed)
        query_grad = grad_query.astype(jnp.bfloat16)
        key_grad = jnp.concatenate([grad_key, grad_value], 1).astype(jnp.bfloat16)
        enc_out_sum = jnp.zeros((head_width, D), jnp.float32)
        enc_qkv_sum = jnp.zeros((D, 3 * head_width), jnp.float32)
        for view_index in range(N_RENDER):
            first = view_index * ROWS
            lat_first = view_index * half_rows
            enc_out_sum = enc_out_sum + to_half(matmul(enc_mixed[lat_first:lat_first + half_rows].T, lat_upstream[lat_first:lat_first + half_rows]))
            query_part = matmul(lat_norm_enc[lat_first:lat_first + half_rows].T, query_grad[lat_first:lat_first + half_rows])
            key_part = matmul(enc_norm[first:first + ROWS].T, key_grad[first:first + ROWS])
            enc_qkv_sum = enc_qkv_sum + to_half(jnp.concatenate([query_part, key_part], 1))
        grad_enc_norm = matmul(key_grad, enc_qkv[:, head_width:].T).reshape(N_RENDER, ROWS, D)
        query_back = matmul(query_grad, enc_qkv[:, :head_width].T).reshape(N_RENDER, half_rows, D)
        grad_enc_norm = grad_enc_norm.at[:, half_rows:].add(query_back).reshape(scene_rows, D).astype(jnp.bfloat16)
        enc_back, enc_gain_term = norm_back(enc_tokens, enc_scale, enc_gain, grad_enc_norm)
        residual = jnp.zeros((N_RENDER, ROWS, D), jnp.float32).at[:, half_rows:].set(lat_upstream.astype(jnp.float32).reshape(N_RENDER, half_rows, D))
        enc_result = (enc_back + residual.reshape(scene_rows, D)).astype(jnp.bfloat16)
        enc_qkv_total, dec_qkv_total, enc_out_total, dec_out_total, enc_gain_total, dec_gain_total = totals
        new_totals = (enc_qkv_total + enc_qkv_sum, dec_qkv_total + dec_qkv_sum, enc_out_total + enc_out_sum, dec_out_total + dec_out_sum, enc_gain_total + enc_gain_term, dec_gain_total + dec_gain_first + dec_gain_second)
        return (new_totals, (enc_result, dec_result))
    initial = (jnp.zeros((D, 3 * head_width), jnp.float32), jnp.zeros((D, 3 * head_width), jnp.float32), jnp.zeros((head_width, D), jnp.float32), jnp.zeros((head_width, D), jnp.float32), jnp.zeros((D,), jnp.float32), jnp.zeros((D,), jnp.float32))
    totals, results = lax.scan(scene_step, initial, (section_tokens[0], section_tokens[1], cotangent))
    token_grads = jnp.stack([results[0], results[1]])
    qkv_grads = jnp.stack([totals[0], totals[1]])
    out_grads = jnp.stack([totals[2], totals[3]])
    gain_grads = jnp.stack([totals[4], totals[5]])
    return (token_grads, qkv_grads, out_grads, gain_grads)
```

```python
import functools

import jax
import jax.numpy as jnp
from jax import lax
from jax.experimental import pallas as pl
from jax.experimental.pallas import tpu as pltpu
from jax.sharding import PartitionSpec as P

HEADS = 8
HD = 128
NORM_EPSILON = 1e-06
BF = jnp.bfloat16
F32 = jnp.float32
MESH = pl.DeviceIdType.MESH
VMEM = pl.BlockSpec(memory_space=pltpu.VMEM)
ANY = pl.BlockSpec(memory_space=pl.ANY)


def dims():
    return lax.axis_size("dp"), lax.axis_size("render")


def ring_index(pos, n):
    return jnp.where(pos < n // 2, 2 * pos, 2 * (n - 1 - pos) + 1)


def ring_position(index, n):
    return jnp.where(index % 2 == 0, index // 2, n - 1 - index // 2)


def pieces_of(out_rows):
    return max(1, min(4, out_rows // 32))


def rows_at(start, size):
    return pl.ds(pl.multiple_of(start, 8), size)


def signal(**where):
    pl.semaphore_signal(
        pltpu.get_barrier_semaphore(), inc=1, device_id=where, device_id_type=MESH
    )


def remote(src, dst, send, recv, **where):
    return pltpu.make_async_remote_copy(
        src_ref=src, dst_ref=dst, send_sem=send, recv_sem=recv,
        device_id=where, device_id_type=MESH,
    )


def call(body, collective_id, outs, in_specs, out_specs, scratch, limit, args):
    return pl.pallas_call(
        body,
        out_shape=outs,
        in_specs=in_specs,
        out_specs=out_specs,
        scratch_shapes=scratch,
        compiler_params=pltpu.CompilerParams(
            collective_id=collective_id, has_side_effects=True, vmem_limit_bytes=limit << 20
        ),
    )(*args)


def gather_kernel(n, count, qw, ow, tok, cot, qfull, ofull, tfull, cfull,
                  local, qsend, qrecv, osend, orecv, tsend, trecv):
    me = lax.axis_index("dp")
    r = lax.axis_index("render")
    pos = ring_position(me, n)
    hop = [ring_index((pos + 1) % n, n), ring_index((pos + n - 1) % n, n)]
    per = n // count
    q_rows, o_rows = qw.shape[0], ow.shape[0]
    pieces = pieces_of(o_rows)
    qr, orr = q_rows // (2 * pieces), o_rows // (2 * pieces)
    t_rows = tok.shape[0]
    for where in hop:
        signal(dp=where)
    for j in range(1, count):
        signal(render=(r + j) % count)
    pl.semaphore_wait(pltpu.get_barrier_semaphore(), 1 + count)

    def q_at(ref, shard, d, k):
        return ref.at[rows_at(shard * q_rows + (d * pieces + k) * qr, qr)]

    def o_at(ref, shard, d, k):
        return ref.at[rows_at((shard % per) * o_rows + (d * pieces + k) * orr, orr)]

    own_out = me // per == r
    keep = [
        pltpu.make_async_copy(qw, qfull.at[rows_at(me * q_rows, q_rows)], local.at[0]),
        pltpu.make_async_copy(tok, tfull.at[rows_at(r * t_rows, t_rows)], local.at[2]),
        pltpu.make_async_copy(cot, cfull.at[rows_at(r * t_rows, t_rows)], local.at[3]),
    ]
    keep_out = pltpu.make_async_copy(
        ow, ofull.at[rows_at((me % per) * o_rows, o_rows)], local.at[1]
    )

    def token_copies(j, sender):
        where = rows_at(sender * t_rows, t_rows)
        peer = (r + j) % count
        return [
            remote(tok, tfull.at[where], tsend.at[0, j], trecv.at[0, j], render=peer),
            remote(cot, cfull.at[where], tsend.at[1, j], trecv.at[1, j], render=peer),
        ]

    for j in range(1, count):
        for c in token_copies(j, r):
            c.start()

    for d in range(2):
        for k in range(pieces):
            remote(qw.at[pl.ds((d * pieces + k) * qr, qr)], q_at(qfull, me, d, k),
                   qsend.at[d, 0, k], qrecv.at[d, 0, k], dp=hop[d]).start()

            @pl.when(own_out)
            def _():
                remote(ow.at[pl.ds((d * pieces + k) * orr, orr)], o_at(ofull, me, d, k),
                       osend.at[d, 0, k], orecv.at[d, 0, k], dp=hop[d]).start()

    for c in keep:
        c.start()

    @pl.when(own_out)
    def _():
        keep_out.start()

    def shard_at(d, s):
        return ring_index((pos + n - s) % n if d == 0 else (pos + s) % n, n)

    def q_copy(d, s, k, shard):
        ref = q_at(qfull, shard, d, k)
        return remote(ref, ref, qsend.at[d, s, k], qrecv.at[d, s, k], dp=hop[d])

    def o_copy(d, s, k, shard):
        ref = o_at(ofull, shard, d, k)
        return remote(ref, ref, osend.at[d, s, k], orecv.at[d, s, k], dp=hop[d])

    def step(s, last):
        for k in range(pieces):
            for d in range(2):
                shard = shard_at(d, s)
                q_copy(d, s - 1, k, shard).wait_recv()
                if not last:
                    q_copy(d, s, k, shard).start()

                @pl.when(shard // per == r)
                def _():
                    o_copy(d, s - 1, k, shard).wait_recv()
                    if not last:
                        o_copy(d, s, k, shard).start()

    @pl.loop(1, n - 1)
    def _(s):
        step(s, False)

    step(n - 1, True)

    @pl.loop(0, n - 1)
    def _(s):
        for k in range(pieces):
            for d in range(2):
                shard = shard_at(d, s)
                q_copy(d, s, k, shard).wait_send()

                @pl.when(shard // per == r)
                def _():
                    o_copy(d, s, k, shard).wait_send()

    for c in keep:
        c.wait()

    @pl.when(own_out)
    def _():
        keep_out.wait()

    for j in range(1, count):
        for c in token_copies(j, (r + count - j) % count):
            c.wait_send()
            c.wait_recv()


def gather(qw, ow, tok, cot):
    n, count = dims()
    pieces = pieces_of(ow.shape[0])
    sem = lambda *shape: pltpu.SemaphoreType.DMA(shape)
    shape = lambda rows, like: jax.ShapeDtypeStruct((rows, like.shape[1]), BF)
    ring = (2, n - 1, pieces)
    return call(
        functools.partial(gather_kernel, n, count), 0,
        (shape(n * qw.shape[0], qw), shape(n // count * ow.shape[0], ow),
         shape(count * tok.shape[0], tok), shape(count * cot.shape[0], cot)),
        [ANY] * 4, (ANY,) * 4,
        [sem(4), sem(*ring), sem(*ring), sem(*ring), sem(*ring), sem(2, count), sem(2, count)],
        16, (qw, ow, tok, cot),
    )


def hop_kernel(source, back, count, part, base, gain, full, gain_out, own, got,
               psend, precv, xsend, xrecv, fsend, frecv):
    r = lax.axis_index("render")
    section = lax.axis_index("section")
    rows = part.shape[0] // count
    for j in range(1, count):
        signal(render=(r + j) % count)
    signal(section=1 - section)
    pl.semaphore_wait(pltpu.get_barrier_semaphore(), count)
    mine = rows_at(r * rows, rows)
    if back:
        gain_out[...] = jnp.zeros_like(gain_out)

    def across():
        return remote(own, full.at[mine], xsend, xrecv, section=1 - source)

    @pl.when(section == source)
    def _():
        def partial(j):
            peer = (r + j) % count
            return remote(part.at[rows_at(peer * rows, rows)], got.at[j - 1],
                          psend.at[j - 1], precv.at[j - 1], render=peer)

        for j in range(1, count):
            partial(j).start()
        total = part[mine].astype(F32)
        for j in range(1, count):
            partial(j).wait_recv()
            total = total + got[j - 1].astype(F32)
        if back:
            grad = total.astype(BF).astype(F32)
            wide = base[mine].astype(F32)
            scale = lax.rsqrt(jnp.mean(wide * wide, axis=-1, keepdims=True) + NORM_EPSILON)
            scaled = grad * gain[...]
            inner = jnp.sum(scaled * wide, axis=-1, keepdims=True)
            own[...] = (
                scale * scaled - wide * (scale**3 * inner / base.shape[-1])
            ).astype(BF)
            gain_out[...] = jnp.sum(grad * wide * scale, axis=0, keepdims=True)
        else:
            own[...] = (base[...].astype(F32) + total).astype(BF)
        across().start()
        across().wait_send()
        for j in range(1, count):
            partial(j).wait_send()
        full[...] = jnp.zeros_like(full)

    @pl.when(section != source)
    def _():
        across().wait_recv()

        def forward(j, sender):
            ref = full.at[rows_at(sender * rows, rows)]
            return remote(ref, ref, fsend.at[j - 1], frecv.at[j - 1], render=(r + j) % count)

        for j in range(1, count):
            forward(j, r).start()
        for j in range(1, count):
            forward(j, r).wait_send()
            forward(j, (r + count - j) % count).wait_recv()


def section_hop(source, back, part, base, gain):
    _, count = dims()
    rows = part.shape[0] // count
    sem = lambda *shape: pltpu.SemaphoreType.DMA(shape)
    return call(
        functools.partial(hop_kernel, source, back, count), 2 if back else 1,
        (jax.ShapeDtypeStruct(part.shape, BF), jax.ShapeDtypeStruct(gain.shape, F32)),
        [VMEM] * 3, (VMEM, VMEM),
        [pltpu.VMEM((rows, part.shape[1]), BF),
         pltpu.VMEM((count - 1, rows, part.shape[1]), BF),
         sem(count - 1), sem(count - 1), pltpu.SemaphoreType.DMA, pltpu.SemaphoreType.DMA,
         sem(count - 1), sem(count - 1)],
        24, (part, base, gain),
    )


def reduce_kernel(n, count, qpart, opart, dpart, tok, resid, gain, gain_lat,
                  qout, oout, tout, gout, qbuf, obuf, dbuf, gbuf, own_gain,
                  qsend, qrecv, osend, orecv, dsend, drecv, gsend, grecv, fsend, frecv, hsend, hrecv):
    me = lax.axis_index("dp")
    r = lax.axis_index("render")
    pos = ring_position(me, n)
    hop = [ring_index((pos + 1) % n, n), ring_index((pos + n - 1) % n, n)]
    per = n // count
    q_rows, o_rows = qpart.shape[0] // n, opart.shape[0] // per
    pieces = pieces_of(o_rows)
    qr, orr = q_rows // (2 * pieces), o_rows // (2 * pieces)
    t_rows = tok.shape[0]
    everyone = n * count
    flat = me * count + r

    @pl.loop(1, everyone)
    def _(j):
        other = (flat + j) % everyone
        signal(dp=other // count, render=other % count)

    pl.semaphore_wait(pltpu.get_barrier_semaphore(), everyone - 1)

    def q_rows_of(shard, d, k):
        return rows_at(shard * q_rows + (d * pieces + k) * qr, qr)

    def o_rows_of(shard, d, k):
        return rows_at((shard % per) * o_rows + (d * pieces + k) * orr, orr)

    def shard_at(d, s):
        return ring_index((pos + 2 * n - 1 - s) % n if d == 0 else (pos + 1 + s) % n, n)

    def q_copy(src, d, s, k):
        return remote(src, qbuf.at[d, s, k], qsend.at[d, s, k], qrecv.at[d, s, k], dp=hop[d])

    def o_copy(src, d, s, k):
        return remote(src, obuf.at[d, s, k], osend.at[d, s, k], orecv.at[d, s, k], dp=hop[d])

    def block(j):
        peer = (r + j) % count
        return remote(dpart.at[rows_at(peer * t_rows, t_rows)], dbuf.at[j - 1],
                      dsend.at[j - 1], drecv.at[j - 1], render=peer)

    for j in range(1, count):
        block(j).start()

    def first(d, k, shard):
        return q_copy(qpart.at[q_rows_of(shard, d, k)], d, 0, k)

    def first_out(d, k, shard):
        return o_copy(opart.at[o_rows_of(shard, d, k)], d, 0, k)

    for k in range(pieces):
        for d in range(2):
            shard = shard_at(d, 0)
            first(d, k, shard).start()

            @pl.when(shard // per == r)
            def _():
                first_out(d, k, shard).start()

    total = dpart[rows_at(r * t_rows, t_rows)].astype(F32)
    for j in range(1, count):
        block(j).wait_recv()
        total = total + dbuf[j - 1].astype(F32)
    grad = total.astype(BF).astype(F32)
    wide = tok[...].astype(F32)
    scale = lax.rsqrt(jnp.mean(wide * wide, axis=-1, keepdims=True) + NORM_EPSILON)
    scaled = grad * gain[...]
    inner = jnp.sum(scaled * wide, axis=-1, keepdims=True)
    tout[...] = (
        resid[...].astype(F32) + scale * scaled - wide * (scale**3 * inner / tok.shape[-1])
    ).astype(BF)
    own_gain[...] = gain_lat[...] + jnp.sum(grad * wide * scale, axis=0, keepdims=True)

    def gain_copy(j, sender):
        other = (flat + j) % everyone
        return remote(own_gain, gbuf.at[sender], gsend.at[j], grecv.at[j],
                      dp=other // count, render=other % count)

    @pl.loop(1, everyone)
    def _(j):
        gain_copy(j, flat).start()

    @pl.loop(1, n - 1)
    def _(s):
        for k in range(pieces):
            for d in range(2):
                shard = shard_at(d, s)
                held = qbuf.at[d, s - 1, k]
                q_copy(held, d, s - 1, k).wait_recv()
                held[...] = (
                    held[...].astype(F32) + qpart[q_rows_of(shard, d, k)].astype(F32)
                ).astype(BF)
                q_copy(held, d, s, k).start()

                @pl.when(shard // per == r)
                def _():
                    held_out = obuf.at[d, s - 1, k]
                    o_copy(held_out, d, s - 1, k).wait_recv()
                    held_out[...] = (
                        held_out[...].astype(F32) + opart[o_rows_of(shard, d, k)].astype(F32)
                    ).astype(BF)
                    o_copy(held_out, d, s, k).start()

    own_out = me // per == r

    def q_final(j, d, k, sender):
        ref = qout.at[sender, pl.ds((d * pieces + k) * qr, qr)]
        return remote(ref, ref, fsend.at[j - 1, d, k], frecv.at[j - 1, d, k],
                      render=(r + j) % count)

    def o_final(j, d, k):
        ref = oout.at[pl.ds((d * pieces + k) * orr, orr)]
        return remote(ref, ref, hsend.at[j - 1, d, k], hrecv.at[d, k], render=(r + j) % count)

    for k in range(pieces):
        for d in range(2):
            held = qbuf.at[d, n - 2, k]
            q_copy(held, d, n - 2, k).wait_recv()
            qout[r, pl.ds((d * pieces + k) * qr, qr)] = (
                held[...].astype(F32) + qpart[q_rows_of(me, d, k)].astype(F32)
            ).astype(BF)
            for j in range(1, count):
                q_final(j, d, k, r).start()

            @pl.when(own_out)
            def _():
                held_out = obuf.at[d, n - 2, k]
                o_copy(held_out, d, n - 2, k).wait_recv()
                oout[pl.ds((d * pieces + k) * orr, orr)] = (
                    held_out[...].astype(F32) + opart[o_rows_of(me, d, k)].astype(F32)
                ).astype(BF)
                for j in range(1, count):
                    o_final(j, d, k).start()

    sums = own_gain[...]
    gbuf[flat] = sums

    @pl.loop(1, everyone)
    def _(j):
        gain_copy(j, (flat + everyone - j) % everyone).wait_recv()
        gain_copy(j, flat).wait_send()

    gout[...] = jnp.sum(gbuf[...], axis=0)

    @pl.loop(0, n - 1)
    def _(s):
        for k in range(pieces):
            for d in range(2):
                shard = shard_at(d, s)
                q_copy(qbuf.at[d, s, k], d, s, k).wait_send()

                @pl.when(shard // per == r)
                def _():
                    o_copy(obuf.at[d, s, k], d, s, k).wait_send()

    for j in range(1, count):
        block(j).wait_send()
        for k in range(pieces):
            for d in range(2):
                q_final(j, d, k, r).wait_send()
                q_final(j, d, k, (r + count - j) % count).wait_recv()

                @pl.when(own_out)
                def _():
                    o_final(j, d, k).wait_send()

    @pl.when(jnp.logical_not(own_out))
    def _():
        for k in range(pieces):
            for d in range(2):
                o_final(1, d, k).wait_recv()


def reduce_all(qpart, opart, dpart, tok, resid, gain, gain_lat):
    n, count = dims()
    per = n // count
    q_rows, o_rows = qpart.shape[0] // n, opart.shape[0] // per
    pieces = pieces_of(o_rows)
    qr, orr = q_rows // (2 * pieces), o_rows // (2 * pieces)
    sem = lambda *shape: pltpu.SemaphoreType.DMA(shape)
    ring = (2, n - 1, pieces)
    return call(
        functools.partial(reduce_kernel, n, count), 3,
        (jax.ShapeDtypeStruct((count, q_rows, qpart.shape[1]), BF),
         jax.ShapeDtypeStruct((o_rows, opart.shape[1]), BF),
         jax.ShapeDtypeStruct(tok.shape, BF),
         jax.ShapeDtypeStruct(gain.shape, F32)),
        [VMEM] * 7, (VMEM,) * 4,
        [pltpu.VMEM(ring + (qr, qpart.shape[1]), BF),
         pltpu.VMEM(ring + (orr, opart.shape[1]), BF),
         pltpu.VMEM((count - 1,) + tok.shape, BF),
         pltpu.VMEM((n * count,) + gain.shape, F32),
         pltpu.VMEM(gain.shape, F32),
         sem(*ring), sem(*ring), sem(*ring), sem(*ring),
         sem(count - 1), sem(count - 1), sem(n * count), sem(n * count),
         sem(count - 1, 2, pieces), sem(count - 1, 2, pieces),
         sem(count - 1, 2, pieces), sem(2, pieces)],
        40, (qpart, opart, dpart, tok, resid, gain, gain_lat),
    )


def rms_norm(values, gain_row):
    wide = values.astype(F32)
    scale = lax.rsqrt(jnp.mean(wide * wide, axis=-1, keepdims=True) + NORM_EPSILON)
    return (wide * scale * gain_row).astype(BF)


def split_heads(values):
    return values.reshape(values.shape[0], -1, HD)


def merge_heads(values):
    return values.reshape(values.shape[0], -1)


def mm(eq, left, right):
    return jnp.einsum(eq, left, right, preferred_element_type=F32)


def softmax_of(queries, key_rows):
    scores = mm("qhd,khd->hqk", split_heads(queries), split_heads(key_rows)) * HD ** (-0.5)
    raised = jnp.exp(scores - jnp.max(scores, axis=-1, keepdims=True))
    return raised / jnp.sum(raised, axis=-1, keepdims=True)


def mixed_of(prob, value_rows):
    return merge_heads(mm("hqk,khd->qhd", prob.astype(BF), split_heads(value_rows))).astype(BF)


def attend_back(queries, key_rows, value_rows, prob, upstream):
    grad_prob = mm("qhd,khd->hqk", split_heads(upstream), split_heads(value_rows))
    delta = jnp.sum(grad_prob * prob, axis=-1, keepdims=True)
    score = (prob * (grad_prob - delta) * HD ** (-0.5)).astype(BF)
    return (
        merge_heads(mm("hqk,khd->qhd", score, split_heads(key_rows))),
        merge_heads(mm("hqk,qhd->khd", score, split_heads(queries))),
        merge_heads(mm("hqk,qhd->khd", prob.astype(BF), split_heads(upstream))),
    )


def only_when(flag, compute):
    def skipped():
        return jax.tree.map(lambda x: jnp.zeros(x.shape, x.dtype), jax.eval_shape(compute))

    return lax.cond(flag, compute, skipped)


def shards(section_tokens, w_qkv, w_out, gains, cotangent):
    n, count = dims()
    tok = section_tokens[0, 0]
    cot = cotangent[0]
    rows = tok.shape[0]
    half = rows // 2
    width = HEADS * HD // count
    is_encoder = lax.axis_index("section") == 0
    r = lax.axis_index("render")
    strips = w_qkv[0].reshape(w_qkv.shape[1], 3, count, width)
    qw = lax.dynamic_index_in_dim(strips, r, 2, keepdims=False).reshape(w_qkv.shape[1], 3 * width)
    qfull, ofull, tfull, cfull = gather(qw, w_out[0], tok, cot)

    normed = rms_norm(tfull, gains)
    proj = jnp.dot(normed, qfull, preferred_element_type=F32).astype(BF)
    keys, values = proj[:, width : 2 * width], proj[:, 2 * width :]

    def latent_rows(x):
        return x.reshape(count, rows, -1)[:, half:].reshape(count * half, -1)

    def encoder_forward():
        mixed = mixed_of(softmax_of(latent_rows(proj[:, :width]), keys), values)
        return mixed, jnp.dot(mixed, ofull, preferred_element_type=F32).astype(BF)

    enc_mixed, zpart = only_when(is_encoder, encoder_forward)
    latent, _ = section_hop(0, False, zpart, tok[half:], gains)

    def decoder_attention():
        lat_norm = rms_norm(latent, gains)
        lat_kv = jnp.dot(lat_norm, qfull[:, width:], preferred_element_type=F32).astype(BF)
        lats = lat_kv.shape[0]
        grad_mixed = mm("nd,cd->nc", cfull, ofull).astype(BF)
        mixeds, grads, lat_sum = [], [], 0.0
        for view in range(count):
            at = slice(view * rows, (view + 1) * rows)
            query = proj[at, :width]
            key_rows = jnp.concatenate([lat_kv[:, :width], keys[at]], 0)
            value_rows = jnp.concatenate([lat_kv[:, width:], values[at]], 0)
            prob = softmax_of(query, key_rows)
            mixeds.append(mixed_of(prob, value_rows))
            dq, dk, dv = attend_back(query, key_rows, value_rows, prob, grad_mixed[at])
            lat_sum = lat_sum + jnp.concatenate([dk[:lats], dv[:lats]], 1)
            grads.append(jnp.concatenate([dq, dk[lats:], dv[lats:]], 1).astype(BF))
        lat_grad = lat_sum.astype(BF)
        dnz = mm("nc,dc->nd", lat_grad, qfull[:, width:]).astype(BF)
        return jnp.concatenate(mixeds, 0), jnp.concatenate(grads, 0), lat_norm, lat_grad, dnz

    dec_mixed, dec_grad, lat_norm, lat_grad, dnz = only_when(
        jnp.logical_not(is_encoder), decoder_attention
    )
    dz, gain_lat = section_hop(1, True, dnz, latent, gains)

    def encoder_back():
        query = latent_rows(proj[:, :width])
        prob = softmax_of(query, keys)
        grad_mixed = mm("nd,cd->nc", dz, ofull).astype(BF)
        opart = mm("nc,nd->cd", enc_mixed, dz).astype(BF)
        dq, dk, dv = attend_back(query, keys, values, prob, grad_mixed)
        dq = dq.astype(BF)
        spread = jnp.pad(dq.reshape(count, half, width), ((0, 0), (half, 0), (0, 0)))
        grad = jnp.concatenate(
            [spread.reshape(count * rows, width), dk.astype(BF), dv.astype(BF)], 1
        )
        qpart = mm("nd,nc->dc", normed, grad).astype(BF)
        dn = mm("nc,dc->nd", grad, qfull).astype(BF)
        own = lax.dynamic_slice_in_dim(dz, r * half, half, 0)
        return qpart, opart, dn, jnp.pad(own, ((half, 0), (0, 0)))

    def decoder_back():
        opart = mm("nc,nd->cd", dec_mixed, cfull).astype(BF)
        both = jnp.concatenate([normed, lat_norm], 0)
        lat_all = jnp.pad(lat_grad, ((0, 0), (width, 0)))
        qpart = mm("nd,nc->dc", both, jnp.concatenate([dec_grad, lat_all], 0)).astype(BF)
        dn = mm("nc,dc->nd", dec_grad, qfull).astype(BF)
        return qpart, opart, dn, cot

    qpart, opart, dn, resid = lax.cond(is_encoder, encoder_back, decoder_back)
    qsum, osum, token_grad, gain_grad = reduce_all(qpart, opart, dn, tok, resid, gains, gain_lat)
    qsum = qsum.reshape(count, -1, 3, width).transpose(1, 2, 0, 3).reshape(w_qkv.shape)
    return (
        token_grad[None, None],
        qsum.astype(F32),
        osum.astype(F32)[None],
        gain_grad,
    )


def solution(mesh):
    in_specs = (
        P("section", "dp", "render", None),
        P("section", "dp", None),
        P("section", "dp", None),
        P("section", None),
        P("dp", "render", None),
    )
    out_specs = (
        P("section", "dp", "render", None),
        P("section", "dp", None),
        P("section", "dp", None),
        P("section", None),
    )
    return jax.shard_map(shards, mesh=mesh, in_specs=in_specs, out_specs=out_specs, check_vma=False)
```

```python
import functools

import jax
import jax.numpy as jnp
from jax import lax
from jax.experimental import pallas as pl
from jax.experimental.pallas import tpu as pltpu
from jax.sharding import PartitionSpec as P

HEADS = 8
HD = 128
NORM_EPSILON = 1e-06
BF = jnp.bfloat16
F32 = jnp.float32
MESH = pl.DeviceIdType.MESH
VMEM = pl.BlockSpec(memory_space=pltpu.VMEM)
ANY = pl.BlockSpec(memory_space=pl.ANY)


def dims():
    return lax.axis_size("dp"), lax.axis_size("render")


def ring_index(pos, n):
    return jnp.where(pos < n // 2, 2 * pos, 2 * (n - 1 - pos) + 1)


def ring_position(index, n):
    return jnp.where(index % 2 == 0, index // 2, n - 1 - index // 2)


def pieces_of(out_rows):
    return max(1, min(4, out_rows // 32))


def rows_at(start, size):
    return pl.ds(pl.multiple_of(start, 8), size)


def signal(**where):
    pl.semaphore_signal(
        pltpu.get_barrier_semaphore(), inc=1, device_id=where, device_id_type=MESH
    )


def remote(src, dst, send, recv, **where):
    return pltpu.make_async_remote_copy(
        src_ref=src, dst_ref=dst, send_sem=send, recv_sem=recv,
        device_id=where, device_id_type=MESH,
    )


def call(body, collective_id, outs, in_specs, out_specs, scratch, limit, args):
    return pl.pallas_call(
        body,
        out_shape=outs,
        in_specs=in_specs,
        out_specs=out_specs,
        scratch_shapes=scratch,
        compiler_params=pltpu.CompilerParams(
            collective_id=collective_id, has_side_effects=True, vmem_limit_bytes=limit << 20
        ),
    )(*args)


def gather_kernel(n, count, qw, ow, tok, cot, qfull, ofull, tfull, cfull,
                  local, qsend, qrecv, osend, orecv, tsend, trecv):
    me = lax.axis_index("dp")
    r = lax.axis_index("render")
    pos = ring_position(me, n)
    hop = [ring_index((pos + 1) % n, n), ring_index((pos + n - 1) % n, n)]
    per = n // count
    q_rows, o_rows = qw.shape[0], ow.shape[0]
    pieces = pieces_of(o_rows)
    qr, orr = q_rows // (2 * pieces), o_rows // (2 * pieces)
    t_rows = tok.shape[0]
    for where in hop:
        signal(dp=where)
    for j in range(1, count):
        signal(render=(r + j) % count)
    pl.semaphore_wait(pltpu.get_barrier_semaphore(), 1 + count)

    def q_at(ref, shard, d, k):
        return ref.at[rows_at(shard * q_rows + (d * pieces + k) * qr, qr)]

    def o_at(ref, shard, d, k):
        return ref.at[rows_at((shard % per) * o_rows + (d * pieces + k) * orr, orr)]

    own_out = me // per == r
    keep = [
        pltpu.make_async_copy(qw, qfull.at[rows_at(me * q_rows, q_rows)], local.at[0]),
        pltpu.make_async_copy(tok, tfull.at[rows_at(r * t_rows, t_rows)], local.at[2]),
        pltpu.make_async_copy(cot, cfull.at[rows_at(r * t_rows, t_rows)], local.at[3]),
    ]
    keep_out = pltpu.make_async_copy(
        ow, ofull.at[rows_at((me % per) * o_rows, o_rows)], local.at[1]
    )

    def token_copies(j, sender):
        where = rows_at(sender * t_rows, t_rows)
        peer = (r + j) % count
        return [
            remote(tok, tfull.at[where], tsend.at[0, j], trecv.at[0, j], render=peer),
            remote(cot, cfull.at[where], tsend.at[1, j], trecv.at[1, j], render=peer),
        ]

    for j in range(1, count):
        for c in token_copies(j, r):
            c.start()

    for d in range(2):
        for k in range(pieces):
            remote(qw.at[pl.ds((d * pieces + k) * qr, qr)], q_at(qfull, me, d, k),
                   qsend.at[d, 0, k], qrecv.at[d, 0, k], dp=hop[d]).start()

            @pl.when(own_out)
            def _():
                remote(ow.at[pl.ds((d * pieces + k) * orr, orr)], o_at(ofull, me, d, k),
                       osend.at[d, 0, k], orecv.at[d, 0, k], dp=hop[d]).start()

    for c in keep:
        c.start()

    @pl.when(own_out)
    def _():
        keep_out.start()

    def shard_at(d, s):
        return ring_index((pos + n - s) % n if d == 0 else (pos + s) % n, n)

    def q_copy(d, s, k, shard):
        ref = q_at(qfull, shard, d, k)
        return remote(ref, ref, qsend.at[d, s, k], qrecv.at[d, s, k], dp=hop[d])

    def o_copy(d, s, k, shard):
        ref = o_at(ofull, shard, d, k)
        return remote(ref, ref, osend.at[d, s, k], orecv.at[d, s, k], dp=hop[d])

    def step(s, last):
        for k in range(pieces):
            for d in range(2):
                shard = shard_at(d, s)
                q_copy(d, s - 1, k, shard).wait_recv()
                if not last:
                    q_copy(d, s, k, shard).start()

                @pl.when(shard // per == r)
                def _():
                    o_copy(d, s - 1, k, shard).wait_recv()
                    if not last:
                        o_copy(d, s, k, shard).start()

    @pl.loop(1, n - 1)
    def _(s):
        step(s, False)

    step(n - 1, True)

    @pl.loop(0, n - 1)
    def _(s):
        for k in range(pieces):
            for d in range(2):
                shard = shard_at(d, s)
                q_copy(d, s, k, shard).wait_send()

                @pl.when(shard // per == r)
                def _():
                    o_copy(d, s, k, shard).wait_send()

    for c in keep:
        c.wait()

    @pl.when(own_out)
    def _():
        keep_out.wait()

    for j in range(1, count):
        for c in token_copies(j, (r + count - j) % count):
            c.wait_send()
            c.wait_recv()


def gather(qw, ow, tok, cot):
    n, count = dims()
    pieces = pieces_of(ow.shape[0])
    sem = lambda *shape: pltpu.SemaphoreType.DMA(shape)
    shape = lambda rows, like: jax.ShapeDtypeStruct((rows, like.shape[1]), BF)
    ring = (2, n - 1, pieces)
    return call(
        functools.partial(gather_kernel, n, count), 0,
        (shape(n * qw.shape[0], qw), shape(n // count * ow.shape[0], ow),
         shape(count * tok.shape[0], tok), shape(count * cot.shape[0], cot)),
        [ANY] * 4, (ANY,) * 4,
        [sem(4), sem(*ring), sem(*ring), sem(*ring), sem(*ring), sem(2, count), sem(2, count)],
        16, (qw, ow, tok, cot),
    )


def dg(left, right, a, b):
    return lax.dot_general(
        left, right, (((a,), (b,)), ((), ())), preferred_element_type=F32
    )


def softmax(queries, keys):
    scores = dg(queries, keys, 1, 1) * HD ** (-0.5)
    raised = jnp.exp(scores - jnp.max(scores, axis=-1, keepdims=True))
    return raised / jnp.sum(raised, axis=-1, keepdims=True)


def score_grad(prob, upstream, values):
    grad_prob = dg(upstream, values, 1, 1)
    delta = jnp.sum(grad_prob * prob, axis=-1, keepdims=True)
    return (prob * (grad_prob - delta) * HD ** (-0.5)).astype(BF)


def inverse_rms(wide):
    return lax.rsqrt(jnp.mean(wide * wide, axis=-1, keepdims=True) + NORM_EPSILON)


def norm_back(wide, gain_row, grad):
    scale = inverse_rms(wide)
    scaled = grad * gain_row
    inner = jnp.sum(scaled * wide, axis=-1, keepdims=True)
    back = scale * scaled - wide * (scale**3 * inner / wide.shape[-1])
    return back, jnp.sum(grad * wide * scale, axis=0, keepdims=True)


def middle_kernel(count, width, tok, gain, proj, ofull, cfull, qfull,
                  dz, gain_lat, lat_norm, lat_grad, dec_mixed, grads, enc_mixed, enc_prob,
                  zfull, part, own, got, wkv, lat_kv, gmix,
                  wsem, psend, precv, xsend, xrecv, fsend, frecv):
    r = lax.axis_index("render")
    section = lax.axis_index("section")
    rows = proj.shape[0] // count
    half = rows // 2
    lats = count * half
    for j in range(1, count):
        signal(render=(r + j) % count)
    signal(section=1 - section)
    mine = rows_at(r * half, half)
    gain_lat[...] = jnp.zeros_like(gain_lat)
    weights = pltpu.make_async_copy(qfull.at[:, pl.ds(width, 2 * width)], wkv, wsem)

    def partial(j):
        return remote(part.at[rows_at((r + j) % count * half, half)], got.at[j - 1],
                      psend.at[j - 1], precv.at[j - 1], render=(r + j) % count)

    def summed():
        for j in range(1, count):
            partial(j).start()
        total = part[mine].astype(F32)
        for j in range(1, count):
            partial(j).wait_recv()
            total = total + got[j - 1].astype(F32)
        return total

    def across(dst):
        return remote(own, dst.at[mine], xsend, xrecv, section=1 - section)

    def leave(dst):
        across(dst).start()
        across(dst).wait_send()
        for j in range(1, count):
            partial(j).wait_send()

    def arrive(dst):
        across(dst).wait_recv()

        def forward(j, sender):
            ref = dst.at[rows_at(sender * half, half)]
            return remote(ref, ref, fsend.at[j - 1], frecv.at[j - 1], render=(r + j) % count)

        for j in range(1, count):
            forward(j, r).start()
        for j in range(1, count):
            forward(j, r).wait_send()
            forward(j, (r + count - j) % count).wait_recv()

    def head(h, strip):
        return pl.ds(strip * width + h * HD, HD)

    @pl.when(section == 0)
    def _():
        for h in range(width // HD):
            query = jnp.concatenate(
                [proj[pl.ds(v * rows + half, half), head(h, 0)] for v in range(count)], 0
            )
            prob = softmax(query, proj[:, head(h, 1)])
            enc_prob[pl.ds(h * lats, lats)] = prob
            enc_mixed[:, head(h, 0)] = dg(prob.astype(BF), proj[:, head(h, 2)], 1, 0).astype(BF)
        part[...] = dg(enc_mixed[...], ofull[...], 1, 0).astype(BF)
        pl.semaphore_wait(pltpu.get_barrier_semaphore(), count)
        own[...] = (tok[pl.ds(half, half)].astype(F32) + summed()).astype(BF)
        leave(zfull)
        arrive(dz)

    @pl.when(section == 1)
    def _():
        weights.start()
        gmix[...] = dg(cfull[...], ofull[...], 1, 1).astype(BF)
        pl.semaphore_wait(pltpu.get_barrier_semaphore(), count)
        weights.wait()
        arrive(zfull)
        wide = zfull[...].astype(F32)
        lat_norm[...] = (wide * inverse_rms(wide) * gain[...]).astype(BF)
        lat_kv[...] = dg(lat_norm[...], wkv[...], 1, 0).astype(BF)
        for h in range(width // HD):
            lat_key = lat_kv[:, head(h, 0)]
            lat_value = lat_kv[:, head(h, 1)]
            key_sum = jnp.zeros((lats, HD), F32)
            value_sum = jnp.zeros((lats, HD), F32)
            for v in range(count):
                at = pl.ds(v * rows, rows)
                query = proj[at, head(h, 0)]
                keys = jnp.concatenate([lat_key, proj[at, head(h, 1)]], 0)
                values = jnp.concatenate([lat_value, proj[at, head(h, 2)]], 0)
                prob = softmax(query, keys)
                rounded = prob.astype(BF)
                dec_mixed[at, head(h, 0)] = dg(rounded, values, 1, 0).astype(BF)
                upstream = gmix[at, head(h, 0)]
                score = score_grad(prob, upstream, values)
                grads[at, head(h, 0)] = dg(score, keys, 1, 0).astype(BF)
                grad_key = dg(score, query, 0, 0)
                grad_value = dg(rounded, upstream, 0, 0)
                grads[at, head(h, 1)] = grad_key[lats:].astype(BF)
                grads[at, head(h, 2)] = grad_value[lats:].astype(BF)
                key_sum = key_sum + grad_key[:lats]
                value_sum = value_sum + grad_value[:lats]
            lat_grad[:, head(h, 0)] = key_sum.astype(BF)
            lat_grad[:, head(h, 1)] = value_sum.astype(BF)
        part[...] = dg(lat_grad[...], wkv[...], 1, 1).astype(BF)
        grad = summed().astype(BF).astype(F32)
        back, gain_term = norm_back(zfull[mine].astype(F32), gain[...], grad)
        own[...] = back.astype(BF)
        gain_lat[...] = gain_term
        leave(dz)


def middle(tok, gain, proj, ofull, cfull, qfull):
    _, count = dims()
    rows, depth = tok.shape
    half = rows // 2
    lats = count * half
    width = proj.shape[1] // 3
    sem = lambda *shape: pltpu.SemaphoreType.DMA(shape)
    out = lambda *shape, t=BF: jax.ShapeDtypeStruct(shape, t)
    return call(
        functools.partial(middle_kernel, count, width), 1,
        (out(lats, depth), out(1, depth, t=F32), out(lats, depth), out(lats, 2 * width),
         out(count * rows, width), out(count * rows, 3 * width), out(lats, width),
         out(width // HD * lats, count * rows, t=F32)),
        [VMEM] * 5 + [ANY], (VMEM,) * 8,
        [pltpu.VMEM((lats, depth), BF), pltpu.VMEM((lats, depth), BF),
         pltpu.VMEM((half, depth), BF), pltpu.VMEM((count - 1, half, depth), BF),
         pltpu.VMEM((depth, 2 * width), BF), pltpu.VMEM((lats, 2 * width), BF),
         pltpu.VMEM((count * rows, width), BF),
         pltpu.SemaphoreType.DMA, sem(count - 1), sem(count - 1),
         pltpu.SemaphoreType.DMA, pltpu.SemaphoreType.DMA, sem(count - 1), sem(count - 1)],
        40, (tok, gain, proj, ofull, cfull, qfull),
    )


def reduce_kernel(n, count, width, norm_t, proj, enc_prob, enc_mixed, dec_mixed, dec_grads, lat_norm,
                  lat_grad, dz, cfull, ofull, tok, gain, gain_lat, qfull,
                  qout, oout, tout, gout,
                  weights, grads, lat_t, gmix, qpart, opart, dpart,
                  qbuf, obuf, dbuf, gbuf, own_gain, wsem,
                  qsend, qrecv, osend, orecv, dsend, drecv, gsend, grecv, fsend, frecv, hsend, hrecv):
    me = lax.axis_index("dp")
    r = lax.axis_index("render")
    section = lax.axis_index("section")
    pos = ring_position(me, n)
    hop = [ring_index((pos + 1) % n, n), ring_index((pos + n - 1) % n, n)]
    per = n // count
    q_rows, o_rows = norm_t.shape[0] // n, opart.shape[0] // per
    pieces = pieces_of(o_rows)
    qr, orr = q_rows // (2 * pieces), o_rows // (2 * pieces)
    t_rows = tok.shape[0]
    half = t_rows // 2
    lats = count * half
    everyone = n * count
    flat = me * count + r
    load = pltpu.make_async_copy(qfull, weights, wsem)
    load.start()

    @pl.loop(1, everyone)
    def _(j):
        other = (flat + j) % everyone
        signal(dp=other // count, render=other % count)

    @pl.when(section == 0)
    def _():
        opart[...] = dg(enc_mixed[...], dz[...], 0, 0).astype(BF)

    @pl.when(section == 1)
    def _():
        opart[...] = dg(dec_mixed[...], cfull[...], 0, 0).astype(BF)
        lat_t[...] = lat_norm[...].T

    pl.semaphore_wait(pltpu.get_barrier_semaphore(), everyone - 1)

    def o_rows_of(shard, d, k):
        return rows_at((shard % per) * o_rows + (d * pieces + k) * orr, orr)

    def shard_at(d, s):
        return ring_index((pos + 2 * n - 1 - s) % n if d == 0 else (pos + 1 + s) % n, n)

    def q_copy(src, d, s, k):
        return remote(src, qbuf.at[d, s, k], qsend.at[d, s, k], qrecv.at[d, s, k], dp=hop[d])

    def o_copy(src, d, s, k):
        return remote(src, obuf.at[d, s, k], osend.at[d, s, k], orecv.at[d, s, k], dp=hop[d])

    def block(j):
        peer = (r + j) % count
        return remote(dpart.at[rows_at(peer * t_rows, t_rows)], dbuf.at[j - 1],
                      dsend.at[j - 1], drecv.at[j - 1], render=peer)

    def o_step(s):
        for k in range(pieces):
            for d in range(2):
                shard = shard_at(d, s)

                @pl.when(shard // per == r)
                def _():
                    held = obuf.at[d, s - 1, k]
                    o_copy(held, d, s - 1, k).wait_recv()
                    held[...] = (
                        held[...].astype(F32) + opart[o_rows_of(shard, d, k)].astype(F32)
                    ).astype(BF)
                    o_copy(held, d, s, k).start()

    for k in range(pieces):
        for d in range(2):
            shard = shard_at(d, 0)

            @pl.when(shard // per == r)
            def _():
                o_copy(opart.at[o_rows_of(shard, d, k)], d, 0, k).start()

    def head(h, strip):
        return pl.ds(strip * width + h * HD, HD)

    @pl.when(section == 0)
    def _():
        gmix[...] = dg(dz[...], ofull[...], 1, 1).astype(BF)
        for v in range(count):
            grads[pl.ds(v * t_rows, half), pl.ds(0, width)] = jnp.zeros((half, width), BF)

    @pl.when(section == 1)
    def _():
        grads[...] = dec_grads[...]

    for h in range(width // HD):
        @pl.when(section == 0)
        def _():
            prob = enc_prob[pl.ds(h * lats, lats)]
            upstream = gmix[:, head(h, 0)]
            query = jnp.concatenate(
                [proj[pl.ds(v * t_rows + half, half), head(h, 0)] for v in range(count)], 0
            )
            score = score_grad(prob, upstream, proj[:, head(h, 2)])
            grad_query = dg(score, proj[:, head(h, 1)], 1, 0).astype(BF)
            for v in range(count):
                grads[pl.ds(v * t_rows + half, half), head(h, 0)] = (
                    grad_query[v * half : (v + 1) * half]
                )
            grads[:, head(h, 1)] = dg(score, query, 0, 0).astype(BF)
            grads[:, head(h, 2)] = dg(prob.astype(BF), upstream, 0, 0).astype(BF)

        if h < n - 2:
            o_step(h + 1)

    def own_part(shard, d):
        at = rows_at(shard * q_rows + d * pieces * qr, pieces * qr)
        term = dg(norm_t[at], grads[...], 1, 0)

        @pl.when(section == 0)
        def _():
            qpart[d] = term.astype(BF)

        @pl.when(section == 1)
        def _():
            lat = dg(lat_t[at], lat_grad[...], 1, 0)
            qpart[d] = jnp.concatenate(
                [term[:, :width], term[:, width:] + lat], 1
            ).astype(BF)

    for d in range(2):
        own_part(shard_at(d, 0), d)
        for k in range(pieces):
            q_copy(qpart.at[d, pl.ds(k * qr, qr)], d, 0, k).start()

    load.wait()
    dpart[...] = dg(grads[...], weights[...], 1, 1).astype(BF)
    for j in range(1, count):
        block(j).start()
    total = dpart[rows_at(r * t_rows, t_rows)].astype(F32)
    for j in range(1, count):
        block(j).wait_recv()
        total = total + dbuf[j - 1].astype(F32)
    back, gain_term = norm_back(tok[...].astype(F32), gain[...], total.astype(BF).astype(F32))
    own_gain[...] = gain_lat[...] + gain_term

    @pl.when(section == 0)
    def _():
        tout[pl.ds(0, half)] = back[:half].astype(BF)
        tout[pl.ds(half, half)] = (back[half:] + dz[rows_at(r * half, half)].astype(F32)).astype(BF)

    @pl.when(section == 1)
    def _():
        tout[...] = (back + cfull[rows_at(r * t_rows, t_rows)].astype(F32)).astype(BF)

    def gain_copy(j, sender):
        other = (flat + j) % everyone
        return remote(own_gain, gbuf.at[sender], gsend.at[j], grecv.at[j],
                      dp=other // count, render=other % count)

    @pl.loop(1, everyone)
    def _(j):
        gain_copy(j, flat).start()

    for d in range(2):
        for k in range(pieces):
            q_copy(qpart.at[d, pl.ds(k * qr, qr)], d, 0, k).wait_send()

    def q_step(s):
        for d in range(2):
            own_part(shard_at(d, s), d)
        for k in range(pieces):
            for d in range(2):
                held = qbuf.at[d, s - 1, k]
                q_copy(held, d, s - 1, k).wait_recv()
                held[...] = (
                    held[...].astype(F32) + qpart[d, pl.ds(k * qr, qr)].astype(F32)
                ).astype(BF)
                q_copy(held, d, s, k).start()

    early = min(width // HD, n - 2)

    @pl.loop(1, n - 1)
    def _(s):
        q_step(s)

        @pl.when(s > early)
        def _():
            o_step(s)

    own_out = me // per == r

    def q_final(j, d, k, sender):
        ref = qout.at[sender, pl.ds((d * pieces + k) * qr, qr)]
        return remote(ref, ref, fsend.at[j - 1, d, k], frecv.at[j - 1, d, k],
                      render=(r + j) % count)

    def o_final(j, d, k):
        ref = oout.at[pl.ds((d * pieces + k) * orr, orr)]
        return remote(ref, ref, hsend.at[j - 1, d, k], hrecv.at[d, k], render=(r + j) % count)

    for d in range(2):
        own_part(me, d)

    for k in range(pieces):
        for d in range(2):
            @pl.when(own_out)
            def _():
                held_out = obuf.at[d, n - 2, k]
                o_copy(held_out, d, n - 2, k).wait_recv()
                oout[pl.ds((d * pieces + k) * orr, orr)] = (
                    held_out[...].astype(F32) + opart[o_rows_of(me, d, k)].astype(F32)
                ).astype(BF)
                for j in range(1, count):
                    o_final(j, d, k).start()

    gbuf[flat] = own_gain[...]

    @pl.loop(1, everyone)
    def _(j):
        gain_copy(j, (flat + everyone - j) % everyone).wait_recv()
        gain_copy(j, flat).wait_send()

    gout[...] = jnp.sum(gbuf[...], axis=0)

    for k in range(pieces):
        for d in range(2):
            held = qbuf.at[d, n - 2, k]
            q_copy(held, d, n - 2, k).wait_recv()
            qout[r, pl.ds((d * pieces + k) * qr, qr)] = (
                held[...].astype(F32) + qpart[d, pl.ds(k * qr, qr)].astype(F32)
            ).astype(BF)
            for j in range(1, count):
                q_final(j, d, k, r).start()

    @pl.loop(0, n - 1)
    def _(s):
        for k in range(pieces):
            for d in range(2):
                shard = shard_at(d, s)

                @pl.when(s > 0)
                def _():
                    q_copy(qbuf.at[d, s, k], d, s, k).wait_send()

                @pl.when(shard // per == r)
                def _():
                    o_copy(obuf.at[d, s, k], d, s, k).wait_send()

    for j in range(1, count):
        block(j).wait_send()
        for k in range(pieces):
            for d in range(2):
                q_final(j, d, k, r).wait_send()
                q_final(j, d, k, (r + count - j) % count).wait_recv()

                @pl.when(own_out)
                def _():
                    o_final(j, d, k).wait_send()

    @pl.when(jnp.logical_not(own_out))
    def _():
        for k in range(pieces):
            for d in range(2):
                o_final(1, d, k).wait_recv()


def reduce_all(*args):
    norm_t, proj, tok, gain = args[0], args[1], args[11], args[12]
    n, count = dims()
    depth = norm_t.shape[0]
    width = proj.shape[1] // 3
    q_rows = depth // n
    o_rows = width * count // n
    pieces = pieces_of(o_rows)
    qr, orr = q_rows // (2 * pieces), o_rows // (2 * pieces)
    lats = tok.shape[0] // 2 * count
    sem = lambda *shape: pltpu.SemaphoreType.DMA(shape)
    ring = (2, n - 1, pieces)
    return call(
        functools.partial(reduce_kernel, n, count, width), 3,
        (jax.ShapeDtypeStruct((count, q_rows, 3 * width), BF),
         jax.ShapeDtypeStruct((o_rows, depth), BF),
         jax.ShapeDtypeStruct(tok.shape, BF),
         jax.ShapeDtypeStruct(gain.shape, F32)),
        [VMEM] * 14 + [ANY], (VMEM,) * 4,
        [pltpu.VMEM((depth, 3 * width), BF), pltpu.VMEM(proj.shape, BF),
         pltpu.VMEM((depth, lats), BF), pltpu.VMEM((lats, width), BF),
         pltpu.VMEM((2, q_rows // 2, 3 * width), BF), pltpu.VMEM((width, depth), BF),
         pltpu.VMEM((proj.shape[0], depth), BF),
         pltpu.VMEM(ring + (qr, 3 * width), BF),
         pltpu.VMEM(ring + (orr, depth), BF),
         pltpu.VMEM((count - 1,) + tok.shape, BF),
         pltpu.VMEM((n * count,) + gain.shape, F32),
         pltpu.VMEM(gain.shape, F32), pltpu.SemaphoreType.DMA,
         sem(*ring), sem(*ring), sem(*ring), sem(*ring),
         sem(count - 1), sem(count - 1), sem(n * count), sem(n * count),
         sem(count - 1, 2, pieces), sem(count - 1, 2, pieces),
         sem(count - 1, 2, pieces), sem(2, pieces)],
        56, args,
    )


def widen_kernel(q_ref, o_ref, qout, oout):
    count, _, wide = q_ref.shape
    width = wide // 3
    for c in range(count):
        for strip in range(3):
            qout[0, :, pl.ds((strip * count + c) * width, width)] = (
                q_ref[c, :, pl.ds(strip * width, width)].astype(F32)
            )
    oout[0] = o_ref[...].astype(F32)


def widen(qsum, osum):
    count, q_rows, wide = qsum.shape
    o_rows, depth = osum.shape
    steps = 4
    qb, ob = q_rows // steps, o_rows // steps
    return pl.pallas_call(
        widen_kernel,
        grid=(steps,),
        out_shape=(jax.ShapeDtypeStruct((1, q_rows, count * wide), F32),
                   jax.ShapeDtypeStruct((1, o_rows, depth), F32)),
        in_specs=[pl.BlockSpec((count, qb, wide), lambda i: (0, i, 0)),
                  pl.BlockSpec((ob, depth), lambda i: (i, 0))],
        out_specs=(pl.BlockSpec((1, qb, count * wide), lambda i: (0, i, 0)),
                   pl.BlockSpec((1, ob, depth), lambda i: (0, i, 0))),
    )(qsum, osum)


def rms_norm(values, gain_row):
    wide = values.astype(F32)
    return (wide * inverse_rms(wide) * gain_row).astype(BF)


def shards(section_tokens, w_qkv, w_out, gains, cotangent):
    n, count = dims()
    tok = section_tokens[0, 0]
    cot = cotangent[0]
    width = HEADS * HD // count
    r = lax.axis_index("render")
    qw = jnp.concatenate(
        [lax.dynamic_slice_in_dim(w_qkv[0], (strip * count + r) * width, width, 1)
         for strip in range(3)], 1
    )
    qfull, ofull, tfull, cfull = gather(qw, w_out[0], tok, cot)
    normed = rms_norm(tfull, gains)
    proj = jnp.dot(normed, qfull, preferred_element_type=F32).astype(BF)
    dz, gain_lat, lat_norm, lat_grad, dec_mixed, dec_grads, enc_mixed, enc_prob = middle(
        tok, gains, proj, ofull, cfull, qfull
    )
    qsum, osum, token_grad, gain_grad = reduce_all(
        normed.T, proj, enc_prob, enc_mixed, dec_mixed, dec_grads, lat_norm, lat_grad,
        dz, cfull, ofull, tok, gains, gain_lat, qfull
    )
    qkv_grad, out_grad = widen(qsum, osum)
    return token_grad[None, None], qkv_grad, out_grad, gain_grad


def solution(mesh):
    in_specs = (
        P("section", "dp", "render", None),
        P("section", "dp", None),
        P("section", "dp", None),
        P("section", None),
        P("dp", "render", None),
    )
    out_specs = (
        P("section", "dp", "render", None),
        P("section", "dp", None),
        P("section", "dp", None),
        P("section", None),
    )
    return jax.shard_map(shards, mesh=mesh, in_specs=in_specs, out_specs=out_specs, check_vma=False)
```

```python
import functools

import jax
import jax.numpy as jnp
from jax import lax
from jax.experimental import pallas as pl
from jax.experimental.pallas import tpu as pltpu
from jax.sharding import PartitionSpec as P

HEADS = 8
HD = 128
NORM_EPSILON = 1e-06
BF = jnp.bfloat16
F32 = jnp.float32
MESH = pl.DeviceIdType.MESH
VMEM = pl.BlockSpec(memory_space=pltpu.VMEM)
ANY = pl.BlockSpec(memory_space=pl.ANY)


def dims():
    return lax.axis_size("dp"), lax.axis_size("render")


def ring_index(pos, n):
    return jnp.where(pos < n // 2, 2 * pos, 2 * (n - 1 - pos) + 1)


def ring_position(index, n):
    return jnp.where(index % 2 == 0, index // 2, n - 1 - index // 2)


def pieces_of(out_rows):
    return max(1, min(4, out_rows // 32))


def rows_at(start, size):
    return pl.ds(pl.multiple_of(start, 8), size)


def signal(**where):
    pl.semaphore_signal(
        pltpu.get_barrier_semaphore(), inc=1, device_id=where, device_id_type=MESH
    )


def remote(src, dst, send, recv, **where):
    return pltpu.make_async_remote_copy(
        src_ref=src, dst_ref=dst, send_sem=send, recv_sem=recv,
        device_id=where, device_id_type=MESH,
    )


def call(body, collective_id, outs, in_specs, out_specs, scratch, limit, args):
    return pl.pallas_call(
        body,
        out_shape=outs,
        in_specs=in_specs,
        out_specs=out_specs,
        scratch_shapes=scratch,
        compiler_params=pltpu.CompilerParams(
            collective_id=collective_id, has_side_effects=True, vmem_limit_bytes=limit << 20
        ),
    )(*args)


def dg(left, right, a, b):
    return lax.dot_general(
        left, right, (((a,), (b,)), ((), ())), preferred_element_type=F32
    )


def softmax(queries, keys):
    scores = dg(queries, keys, 1, 1) * HD ** (-0.5)
    raised = jnp.exp(scores - jnp.max(scores, axis=-1, keepdims=True))
    return raised / jnp.sum(raised, axis=-1, keepdims=True)


def score_grad(prob, upstream, values):
    grad_prob = dg(upstream, values, 1, 1)
    delta = jnp.sum(grad_prob * prob, axis=-1, keepdims=True)
    return (prob * (grad_prob - delta) * HD ** (-0.5)).astype(BF)


def inverse_rms(wide):
    return lax.rsqrt(jnp.mean(wide * wide, axis=-1, keepdims=True) + NORM_EPSILON)


def norm_back(wide, gain_row, grad):
    scale = inverse_rms(wide)
    scaled = grad * gain_row
    inner = jnp.sum(scaled * wide, axis=-1, keepdims=True)
    back = scale * scaled - wide * (scale**3 * inner / wide.shape[-1])
    return back, jnp.sum(grad * wide * scale, axis=0, keepdims=True)


def step_kernel(n, count, width, qw, ow, tok, cot, gain,
                qout, oout, tout, gout,
                qfull, ofull, tfull, cfull, norm_t, acc, proj, enc_prob, mixed, gmix,
                lat_norm, lat_t, lat_kv, lat_grad, grads, zfull, dz, part, own, got, gain_lat,
                qpart, opart, dpart, qbuf, obuf, dbuf, gbuf, own_gain,
                gqs, gqr, gos, gor, tsend, trecv, psend, precv, xsend, xrecv, fsend, frecv,
                qsend, qrecv, osend, orecv, dsend, drecv, gsend, grecv, esend, erecv, hsend, hrecv):
    me = lax.axis_index("dp")
    r = lax.axis_index("render")
    section = lax.axis_index("section")
    pos = ring_position(me, n)
    hop = [ring_index((pos + 1) % n, n), ring_index((pos + n - 1) % n, n)]
    per = n // count
    q_rows, o_rows = qw.shape[0], ow.shape[0]
    pieces = pieces_of(o_rows)
    qr, orr = q_rows // (2 * pieces), o_rows // (2 * pieces)
    side = q_rows // 2
    rows = tok.shape[0]
    half = rows // 2
    lats = count * half
    heads = width // HD
    wide_head = 3 * HD
    everyone = n * count
    flat = me * count + r
    own_out = me // per == r
    mine = rows_at(r * half, half)
    barrier = pltpu.get_barrier_semaphore()

    @pl.loop(1, everyone)
    def _(j):
        other = (flat + j) % everyone
        signal(dp=other // count, render=other % count)

    signal(section=1 - section)
    pl.semaphore_wait(barrier, everyone)

    def head(h, strip):
        return pl.ds(h * wide_head + strip * HD, HD)

    def pair(h):
        return pl.ds(h * wide_head + HD, 2 * HD)


    def q_at(shard, d, k):
        return qfull.at[rows_at(shard * q_rows + (d * pieces + k) * qr, qr)]

    def o_rows_of(shard, d, k):
        return rows_at((shard % per) * o_rows + (d * pieces + k) * orr, orr)

    def token_copies(j, sender):
        where = rows_at(sender * rows, rows)
        peer = (r + j) % count
        return [
            remote(tok, tfull.at[where], tsend.at[0, j - 1], trecv.at[0, j - 1], render=peer),
            remote(cot, cfull.at[where], tsend.at[1, j - 1], trecv.at[1, j - 1], render=peer),
        ]

    for j in range(1, count):
        for c in token_copies(j, r):
            c.start()

    def first_q(d, k):
        return remote(qw.at[pl.ds((d * pieces + k) * qr, qr)], q_at(me, d, k),
                      gqs.at[d, 0, k], gqr.at[d, 0, k], dp=hop[d])

    def first_o(d, k):
        return remote(ow.at[pl.ds((d * pieces + k) * orr, orr)], ofull.at[o_rows_of(me, d, k)],
                      gos.at[d, 0, k], gor.at[d, 0, k], dp=hop[d])

    for k in range(pieces):
        for d in range(2):
            first_q(d, k).start()

    for k in range(pieces):
        for d in range(2):
            @pl.when(own_out)
            def _():
                first_o(d, k).start()

    def origin(d, s):
        return ring_index((pos + n - s) % n if d == 0 else (pos + s) % n, n)

    def q_in(d, s, k):
        ref = q_at(origin(d, s), d, k)
        return remote(ref, ref, gqs.at[d, s - 1, k], gqr.at[d, s - 1, k], dp=hop[d])

    def q_on(d, s, k):
        ref = q_at(origin(d, s), d, k)
        return remote(ref, ref, gqs.at[d, s, k], gqr.at[d, s, k], dp=hop[d])

    def o_in(d, s, k):
        ref = ofull.at[o_rows_of(origin(d, s), d, k)]
        return remote(ref, ref, gos.at[d, s - 1, k], gor.at[d, s - 1, k], dp=hop[d])

    def o_on(d, s, k):
        ref = ofull.at[o_rows_of(origin(d, s), d, k)]
        return remote(ref, ref, gos.at[d, s, k], gor.at[d, s, k], dp=hop[d])

    def q_forward(s, last):
        for k in range(pieces):
            for d in range(2):
                q_in(d, s, k).wait_recv()
                if not last:
                    q_on(d, s, k).start()

    def o_forward(s, last):
        for k in range(pieces):
            for d in range(2):
                @pl.when(origin(d, s) // per == r)
                def _():
                    o_in(d, s, k).wait_recv()
                    if not last:
                        o_on(d, s, k).start()

    def project(s):
        for d in range(2):
            at = rows_at(origin(d, s) * q_rows + d * side, side)
            acc[...] += dg(norm_t[at], qfull[at], 0, 0)

    qfull[rows_at(me * q_rows, q_rows)] = qw[...]

    @pl.when(own_out)
    def _():
        ofull[rows_at((me % per) * o_rows, o_rows)] = ow[...]

    tfull[rows_at(r * rows, rows)] = tok[...]
    cfull[rows_at(r * rows, rows)] = cot[...]
    for j in range(1, count):
        for c in token_copies(j, (r + count - j) % count):
            c.wait_recv()
    for v in range(count):
        wide = tfull[pl.ds(v * rows, rows)].astype(F32)
        norm_t[:, pl.ds(v * rows, rows)] = (
            (wide * inverse_rms(wide) * gain[...]).astype(BF).T
        )
    acc[...] = jnp.zeros_like(acc)
    project(0)
    lag = min(2, n - 2)

    @pl.loop(1, n - 1)
    def _(s):
        q_forward(s, False)

        @pl.when(s > lag)
        def _():
            o_forward(s - lag, False)

        project(s)

    q_forward(n - 1, True)
    late = list(range(n - 1 - lag, n))
    o_forward(late[0], late[0] == n - 1)
    project(n - 1)
    proj[...] = acc[...].astype(BF)
    late = late[1:]

    for h in range(heads):
        @pl.when(section == 0)
        def _():
            query = jnp.concatenate(
                [proj[pl.ds(v * rows + half, half), head(h, 0)] for v in range(count)], 0
            )
            prob = softmax(query, proj[:, head(h, 1)])
            enc_prob[pl.ds(h * lats, lats)] = prob
            mixed[pl.ds(0, lats), pl.ds(h * HD, HD)] = dg(
                prob.astype(BF), proj[:, head(h, 2)], 1, 0
            ).astype(BF)

        if late:
            s = late.pop(0)
            o_forward(s, s == n - 1)
    for s in late:
        o_forward(s, s == n - 1)


    def partial(j):
        return remote(part.at[rows_at((r + j) % count * half, half)], got.at[j - 1],
                      psend.at[j - 1], precv.at[j - 1], render=(r + j) % count)

    def summed():
        for j in range(1, count):
            partial(j).start()
        total = part[mine].astype(F32)
        for j in range(1, count):
            partial(j).wait_recv()
            total = total + got[j - 1].astype(F32)
        return total

    def across(dst):
        return remote(own, dst.at[mine], xsend, xrecv, section=1 - section)

    def arrive(dst):
        across(dst).wait_recv()

        def forward(j, sender):
            ref = dst.at[rows_at(sender * half, half)]
            return remote(ref, ref, fsend.at[j - 1], frecv.at[j - 1], render=(r + j) % count)

        for j in range(1, count):
            forward(j, r).start()
        for j in range(1, count):
            forward(j, r).wait_send()
            forward(j, (r + count - j) % count).wait_recv()

    @pl.when(section == 0)
    def _():
        gain_lat[...] = jnp.zeros_like(gain_lat)
        part[...] = dg(mixed[pl.ds(0, lats)], ofull[...], 1, 0).astype(BF)
        own[...] = (tok[pl.ds(half, half)].astype(F32) + summed()).astype(BF)
        across(zfull).start()
        arrive(dz)
        opart[...] = dg(mixed[pl.ds(0, lats)], dz[...], 0, 0).astype(BF)

    @pl.when(section == 1)
    def _():
        gmix[...] = dg(cfull[...], ofull[...], 1, 1).astype(BF)
        arrive(zfull)
        wide = zfull[...].astype(F32)
        lat_norm[...] = (wide * inverse_rms(wide) * gain[...]).astype(BF)
        for h in range(heads):
            both = pl.ds(h * 2 * HD, 2 * HD)
            lat_kv[:, both] = dg(lat_norm[...], qfull[:, pair(h)], 1, 0).astype(BF)
        total = None
        for h in range(heads):
            lat_key = lat_kv[:, pl.ds(h * 2 * HD, HD)]
            lat_value = lat_kv[:, pl.ds(h * 2 * HD + HD, HD)]
            key_sum = jnp.zeros((lats, HD), F32)
            value_sum = jnp.zeros((lats, HD), F32)
            for v in range(count):
                at = pl.ds(v * rows, rows)
                query = proj[at, head(h, 0)]
                keys = jnp.concatenate([lat_key, proj[at, head(h, 1)]], 0)
                values = jnp.concatenate([lat_value, proj[at, head(h, 2)]], 0)
                prob = softmax(query, keys)
                rounded = prob.astype(BF)
                mixed[at, pl.ds(h * HD, HD)] = dg(rounded, values, 1, 0).astype(BF)
                upstream = gmix[at, pl.ds(h * HD, HD)]
                score = score_grad(prob, upstream, values)
                grads[at, head(h, 0)] = dg(score, keys, 1, 0).astype(BF)
                grad_key = dg(score, query, 0, 0)
                grad_value = dg(rounded, upstream, 0, 0)
                grads[at, head(h, 1)] = grad_key[lats:].astype(BF)
                grads[at, head(h, 2)] = grad_value[lats:].astype(BF)
                key_sum = key_sum + grad_key[:lats]
                value_sum = value_sum + grad_value[:lats]
            lat_grad[:, pl.ds(h * 2 * HD, HD)] = key_sum.astype(BF)
            lat_grad[:, pl.ds(h * 2 * HD + HD, HD)] = value_sum.astype(BF)
        total = dg(lat_grad[:, pl.ds(0, 2 * HD)], qfull[:, pair(0)], 1, 1)
        for h in range(1, heads):
            total = total + dg(lat_grad[:, pl.ds(h * 2 * HD, 2 * HD)], qfull[:, pair(h)], 1, 1)
        part[...] = total.astype(BF)
        grad = summed().astype(BF).astype(F32)
        back, gain_term = norm_back(zfull[mine].astype(F32), gain[...], grad)
        own[...] = back.astype(BF)
        gain_lat[...] = gain_term
        across(dz).start()
        opart[...] = dg(mixed[...], cfull[...], 0, 0).astype(BF)
        lat_t[...] = lat_norm[...].T


    def shard_at(d, s):
        return ring_index((pos + 2 * n - 1 - s) % n if d == 0 else (pos + 1 + s) % n, n)

    def q_copy(src, d, s, h):
        return remote(src, qbuf.at[d, s, h], qsend.at[d, s, h], qrecv.at[d, s, h], dp=hop[d])

    def o_copy(src, d, s, k):
        return remote(src, obuf.at[d, s, k], osend.at[d, s, k], orecv.at[d, s, k], dp=hop[d])

    def o_first(d, k):
        return o_copy(opart.at[o_rows_of(shard_at(d, 0), d, k)], d, 0, k)

    for k in range(pieces):
        for d in range(2):
            @pl.when(shard_at(d, 0) // per == r)
            def _():
                o_first(d, k).start()

    def own_term(shard, d, h):
        at = rows_at(shard * q_rows + d * side, side)
        qpart[d, h] = dg(norm_t[at], grads[:, pl.ds(h * wide_head, wide_head)], 1, 0)

        @pl.when(section == 1)
        def _():
            lat = dg(lat_t[at], lat_grad[:, pl.ds(h * 2 * HD, 2 * HD)], 1, 0)
            qpart[d, h, :, pl.ds(HD, 2 * HD)] += lat

    @pl.when(section == 0)
    def _():
        gmix[pl.ds(0, lats)] = dg(dz[...], ofull[...], 1, 1).astype(BF)

    for h in range(heads):
        @pl.when(section == 0)
        def _():
            prob = enc_prob[pl.ds(h * lats, lats)]
            upstream = gmix[pl.ds(0, lats), pl.ds(h * HD, HD)]
            query = jnp.concatenate(
                [proj[pl.ds(v * rows + half, half), head(h, 0)] for v in range(count)], 0
            )
            score = score_grad(prob, upstream, proj[:, head(h, 2)])
            grad_query = dg(score, proj[:, head(h, 1)], 1, 0).astype(BF)
            for v in range(count):
                grads[pl.ds(v * rows, half), head(h, 0)] = jnp.zeros((half, HD), BF)
                grads[pl.ds(v * rows + half, half), head(h, 0)] = (
                    grad_query[v * half : (v + 1) * half]
                )
            grads[:, head(h, 1)] = dg(score, query, 0, 0).astype(BF)
            grads[:, head(h, 2)] = dg(prob.astype(BF), upstream, 0, 0).astype(BF)

        for d in range(2):
            own_term(shard_at(d, 0), d, h)
            qbuf[d, n - 1, h] = qpart[d, h].astype(BF)
            q_copy(qbuf.at[d, n - 1, h], d, 0, h).start()

    dpart[...] = dg(grads[...], qfull[...], 1, 1).astype(BF)

    def block(j):
        peer = (r + j) % count
        return remote(dpart.at[rows_at(peer * rows, rows)], dbuf.at[j - 1],
                      dsend.at[j - 1], drecv.at[j - 1], render=peer)

    for j in range(1, count):
        block(j).start()
    total = dpart[rows_at(r * rows, rows)].astype(F32)
    for j in range(1, count):
        block(j).wait_recv()
        total = total + dbuf[j - 1].astype(F32)
    back, gain_term = norm_back(tok[...].astype(F32), gain[...], total.astype(BF).astype(F32))
    own_gain[...] = gain_lat[...] + gain_term

    @pl.when(section == 0)
    def _():
        tout[pl.ds(0, half)] = back[:half].astype(BF)
        tout[pl.ds(half, half)] = (back[half:] + dz[mine].astype(F32)).astype(BF)

    @pl.when(section == 1)
    def _():
        tout[...] = (back + cot[...].astype(F32)).astype(BF)

    def gain_copy(j, sender):
        other = (flat + j) % everyone
        return remote(own_gain, gbuf.at[sender], gsend.at[j], grecv.at[j],
                      dp=other // count, render=other % count)

    @pl.loop(1, everyone)
    def _(j):
        gain_copy(j, flat).start()

    @pl.loop(1, n - 1)
    def _(s):
        for h in range(heads):
            for d in range(2):
                own_term(shard_at(d, s), d, h)
        for h in range(heads):
            for d in range(2):
                held = qbuf.at[d, s - 1, h]
                q_copy(held, d, s - 1, h).wait_recv()
                held[...] = (held[...].astype(F32) + qpart[d, h]).astype(BF)
                q_copy(held, d, s, h).start()
        for k in range(pieces):
            for d in range(2):
                shard = shard_at(d, s)

                @pl.when(shard // per == r)
                def _():
                    held = obuf.at[d, s - 1, k]
                    o_copy(held, d, s - 1, k).wait_recv()
                    held[...] = (
                        held[...].astype(F32) + opart[o_rows_of(shard, d, k)].astype(F32)
                    ).astype(BF)
                    o_copy(held, d, s, k).start()

    def q_final(j, d, h, sender):
        ref = qout.at[sender, pl.ds(d * side, side), pl.ds(h * wide_head, wide_head)]
        return remote(ref, ref, esend.at[j - 1, d, h], erecv.at[j - 1, d, h],
                      render=(r + j) % count)

    def o_final(j, d, k):
        ref = oout.at[pl.ds((d * pieces + k) * orr, orr)]
        return remote(ref, ref, hsend.at[j - 1, d, k], hrecv.at[d, k], render=(r + j) % count)

    for h in range(heads):
        for d in range(2):
            own_term(me, d, h)

    gbuf[flat] = own_gain[...]

    @pl.loop(1, everyone)
    def _(j):
        gain_copy(j, (flat + everyone - j) % everyone).wait_recv()
        gain_copy(j, flat).wait_send()

    gout[...] = jnp.sum(gbuf[...], axis=0)

    for h in range(heads):
        for d in range(2):
            held = qbuf.at[d, n - 2, h]
            q_copy(held, d, n - 2, h).wait_recv()
            qout[r, pl.ds(d * side, side), pl.ds(h * wide_head, wide_head)] = (
                held[...].astype(F32) + qpart[d, h]
            ).astype(BF)
            for j in range(1, count):
                q_final(j, d, h, r).start()

    for k in range(pieces):
        for d in range(2):
            @pl.when(own_out)
            def _():
                held = obuf.at[d, n - 2, k]
                o_copy(held, d, n - 2, k).wait_recv()
                oout[pl.ds((d * pieces + k) * orr, orr)] = (
                    held[...].astype(F32) + opart[o_rows_of(me, d, k)].astype(F32)
                ).astype(BF)
                for j in range(1, count):
                    o_final(j, d, k).start()


    @pl.loop(0, n - 1)
    def _(s):
        for d in range(2):
            for h in range(heads):
                q_copy(qbuf.at[d, s, h], d, s, h).wait_send()
            for k in range(pieces):
                q_on(d, s, k).wait_send()

                @pl.when(origin(d, s) // per == r)
                def _():
                    o_on(d, s, k).wait_send()

                @pl.when(shard_at(d, s) // per == r)
                def _():
                    o_copy(obuf.at[d, s, k], d, s, k).wait_send()

    across(dz).wait_send()
    for j in range(1, count):
        for c in token_copies(j, r):
            c.wait_send()
        partial(j).wait_send()
        block(j).wait_send()
        for d in range(2):
            for h in range(heads):
                q_final(j, d, h, r).wait_send()
                q_final(j, d, h, (r + count - j) % count).wait_recv()
            for k in range(pieces):
                @pl.when(own_out)
                def _():
                    o_final(j, d, k).wait_send()

    @pl.when(jnp.logical_not(own_out))
    def _():
        for k in range(pieces):
            for d in range(2):
                o_final(1, d, k).wait_recv()


def whole_step(qw, ow, tok, cot, gain):
    n, count = dims()
    q_rows, wide = qw.shape
    o_rows, depth = ow.shape
    width = wide // 3
    heads = width // HD
    pieces = pieces_of(o_rows)
    orr = o_rows // (2 * pieces)
    rows = tok.shape[0]
    half = rows // 2
    lats = half * count
    scene = rows * count
    everyone = n * count
    sem = lambda *shape: pltpu.SemaphoreType.DMA(shape)
    one = pltpu.SemaphoreType.DMA
    mem = lambda *shape, t=BF: pltpu.VMEM(shape, t)
    ring = (2, n - 1, pieces)
    turn = (2, n - 1, heads)
    return call(
        functools.partial(step_kernel, n, count, width), 0,
        (jax.ShapeDtypeStruct((count, q_rows, wide), BF),
         jax.ShapeDtypeStruct((o_rows, depth), BF),
         jax.ShapeDtypeStruct(tok.shape, BF),
         jax.ShapeDtypeStruct(gain.shape, F32)),
        [VMEM] * 5, (VMEM,) * 4,
        [mem(depth, wide), mem(width, depth), mem(scene, depth), mem(scene, depth),
         mem(depth, scene), mem(scene, wide, t=F32), mem(scene, wide),
         mem(heads * lats, scene, t=F32), mem(scene, width), mem(scene, width),
         mem(lats, depth), mem(depth, lats), mem(lats, 2 * width), mem(lats, 2 * width),
         mem(scene, wide), mem(lats, depth), mem(lats, depth), mem(lats, depth),
         mem(half, depth), mem(count - 1, half, depth), mem(1, depth, t=F32),
         mem(2, heads, q_rows // 2, 3 * HD, t=F32), mem(width, depth), mem(scene, depth),
         mem(2, n, heads, q_rows // 2, 3 * HD), mem(*ring, orr, depth),
         mem(count - 1, rows, depth), mem(everyone, 1, depth, t=F32), mem(1, depth, t=F32),
         sem(*ring), sem(*ring), sem(*ring), sem(*ring),
         sem(2, count - 1), sem(2, count - 1), sem(count - 1), sem(count - 1),
         one, one, sem(count - 1), sem(count - 1),
         sem(*turn), sem(*turn), sem(*ring), sem(*ring),
         sem(count - 1), sem(count - 1), sem(everyone), sem(everyone),
         sem(count - 1, 2, heads), sem(count - 1, 2, heads),
         sem(count - 1, 2, pieces), sem(2, pieces)],
        60, (qw, ow, tok, cot, gain),
    )


def widen_kernel(q_ref, o_ref, qout, oout):
    count, _, wide = q_ref.shape
    width = wide // 3
    for c in range(count):
        for strip in range(3):
            for h in range(width // HD):
                qout[0, :, pl.ds((strip * count + c) * width + h * HD, HD)] = (
                    q_ref[c, :, pl.ds((3 * h + strip) * HD, HD)].astype(F32)
                )
    oout[0] = o_ref[...].astype(F32)


def widen(qsum, osum):
    count, q_rows, wide = qsum.shape
    o_rows, depth = osum.shape
    steps = 4
    qb, ob = q_rows // steps, o_rows // steps
    return pl.pallas_call(
        widen_kernel,
        grid=(steps,),
        out_shape=(jax.ShapeDtypeStruct((1, q_rows, count * wide), F32),
                   jax.ShapeDtypeStruct((1, o_rows, depth), F32)),
        in_specs=[pl.BlockSpec((count, qb, wide), lambda i: (0, i, 0)),
                  pl.BlockSpec((ob, depth), lambda i: (i, 0))],
        out_specs=(pl.BlockSpec((1, qb, count * wide), lambda i: (0, i, 0)),
                   pl.BlockSpec((1, ob, depth), lambda i: (0, i, 0))),
    )(qsum, osum)


def shards(section_tokens, w_qkv, w_out, gains, cotangent):
    n, count = dims()
    width = HEADS * HD // count
    r = lax.axis_index("render")
    qw = jnp.concatenate(
        [lax.dynamic_slice_in_dim(w_qkv[0], (strip * count + r) * width + h * HD, HD, 1)
         for h in range(width // HD) for strip in range(3)], 1
    )
    qsum, osum, token_grad, gain_grad = whole_step(
        qw, w_out[0], section_tokens[0, 0], cotangent[0], gains
    )
    qkv_grad, out_grad = widen(qsum, osum)
    return token_grad[None, None], qkv_grad, out_grad, gain_grad


def solution(mesh):
    in_specs = (
        P("section", "dp", "render", None),
        P("section", "dp", None),
        P("section", "dp", None),
        P("section", None),
        P("dp", "render", None),
    )
    out_specs = (
        P("section", "dp", "render", None),
        P("section", "dp", None),
        P("section", "dp", None),
        P("section", None),
    )
    return jax.shard_map(shards, mesh=mesh, in_specs=in_specs, out_specs=out_specs, check_vma=False)
```

```python
import functools

import jax
import jax.numpy as jnp
from jax import lax
from jax.experimental import pallas as pl
from jax.experimental.pallas import tpu as pltpu
from jax.sharding import PartitionSpec as P

HEADS = 8
HD = 128
NORM_EPSILON = 1e-06
BF = jnp.bfloat16
F32 = jnp.float32
MESH = pl.DeviceIdType.MESH
VMEM = pl.BlockSpec(memory_space=pltpu.VMEM)
ANY = pl.BlockSpec(memory_space=pl.ANY)


def dims():
    return lax.axis_size("dp"), lax.axis_size("render")


def ring_index(pos, n):
    return jnp.where(pos < n // 2, 2 * pos, 2 * (n - 1 - pos) + 1)


def ring_position(index, n):
    return jnp.where(index % 2 == 0, index // 2, n - 1 - index // 2)


def pieces_of(out_rows):
    return max(1, min(4, out_rows // 32))


def rows_at(start, size):
    return pl.ds(pl.multiple_of(start, 8), size)


def signal(**where):
    pl.semaphore_signal(
        pltpu.get_barrier_semaphore(), inc=1, device_id=where, device_id_type=MESH
    )


def remote(src, dst, send, recv, **where):
    return pltpu.make_async_remote_copy(
        src_ref=src, dst_ref=dst, send_sem=send, recv_sem=recv,
        device_id=where, device_id_type=MESH,
    )


def call(body, collective_id, outs, in_specs, out_specs, scratch, limit, args):
    return pl.pallas_call(
        body,
        out_shape=outs,
        in_specs=in_specs,
        out_specs=out_specs,
        scratch_shapes=scratch,
        compiler_params=pltpu.CompilerParams(
            collective_id=collective_id, has_side_effects=True, vmem_limit_bytes=limit << 20
        ),
    )(*args)


def dg(left, right, a, b):
    return lax.dot_general(
        left, right, (((a,), (b,)), ((), ())), preferred_element_type=F32
    )


def softmax(queries, keys):
    scores = dg(queries, keys, 1, 1) * HD ** (-0.5)
    raised = jnp.exp(scores - jnp.max(scores, axis=-1, keepdims=True))
    return raised / jnp.sum(raised, axis=-1, keepdims=True)


def score_grad(prob, upstream, values):
    grad_prob = dg(upstream, values, 1, 1)
    delta = jnp.sum(grad_prob * prob, axis=-1, keepdims=True)
    return (prob * (grad_prob - delta) * HD ** (-0.5)).astype(BF)


def inverse_rms(wide):
    return lax.rsqrt(jnp.mean(wide * wide, axis=-1, keepdims=True) + NORM_EPSILON)


def norm_back(wide, gain_row, grad):
    scale = inverse_rms(wide)
    scaled = grad * gain_row
    inner = jnp.sum(scaled * wide, axis=-1, keepdims=True)
    back = scale * scaled - wide * (scale**3 * inner / wide.shape[-1])
    return back, jnp.sum(grad * wide * scale, axis=0, keepdims=True)


def step_kernel(n, count, width, w, ow, tok, cot, gain,
                qout, oout, tout, gout,
                qfull, ofull, tfull, cfull, norm_t, acc, proj, enc_prob, mixed, gmix,
                lat_norm, lat_t, lat_kv, lat_grad, grads, zfull, dz, part, own, got, gain_lat,
                qpart, opart, dpart, qbuf, obuf, dbuf, gbuf, own_gain, wsem,
                gqs, gqr, gos, gor, tsend, trecv, psend, precv, xsend, xrecv, fsend, frecv,
                qsend, qrecv, osend, orecv, dsend, drecv, gsend, grecv, esend, erecv, hsend, hrecv):
    me = lax.axis_index("dp")
    r = lax.axis_index("render")
    section = lax.axis_index("section")
    pos = ring_position(me, n)
    hop = [ring_index((pos + 1) % n, n), ring_index((pos + n - 1) % n, n)]
    per = n // count
    q_rows, o_rows = w.shape[0], ow.shape[0]
    pieces = pieces_of(o_rows)
    qr, orr = q_rows // (2 * pieces), o_rows // (2 * pieces)
    side = q_rows // 2
    rows = tok.shape[0]
    half = rows // 2
    lats = count * half
    heads = width // HD
    wide_head = 3 * HD
    everyone = n * count
    flat = me * count + r
    own_out = me // per == r
    mine = rows_at(r * half, half)
    barrier = pltpu.get_barrier_semaphore()

    def columns(h, strip):
        start = pl.multiple_of((strip * count + r) * width + h * HD, HD)
        return pltpu.make_async_copy(
            w.at[:, pl.ds(start, HD)],
            qfull.at[rows_at(me * q_rows, q_rows), pl.ds(h * 3 * HD + strip * HD, HD)],
            wsem.at[h, strip],
        )

    strips = [columns(h, strip) for h in range(heads) for strip in range(3)]
    for c in strips:
        c.start()

    @pl.loop(1, everyone)
    def _(j):
        other = (flat + j) % everyone
        signal(dp=other // count, render=other % count)

    signal(section=1 - section)
    pl.semaphore_wait(barrier, everyone)

    def head(h, strip):
        return pl.ds(h * wide_head + strip * HD, HD)

    def pair(h):
        return pl.ds(h * wide_head + HD, 2 * HD)


    def q_at(shard, d, k):
        return qfull.at[rows_at(shard * q_rows + (d * pieces + k) * qr, qr)]

    def o_rows_of(shard, d, k):
        return rows_at((shard % per) * o_rows + (d * pieces + k) * orr, orr)

    def token_copies(j, sender):
        where = rows_at(sender * rows, rows)
        peer = (r + j) % count
        return [
            remote(tok, tfull.at[where], tsend.at[0, j - 1], trecv.at[0, j - 1], render=peer),
            remote(cot, cfull.at[where], tsend.at[1, j - 1], trecv.at[1, j - 1], render=peer),
        ]

    for j in range(1, count):
        for c in token_copies(j, r):
            c.start()

    def first_q(d, k):
        return remote(q_at(me, d, k), q_at(me, d, k),
                      gqs.at[d, 0, k], gqr.at[d, 0, k], dp=hop[d])

    def first_o(d, k):
        return remote(ow.at[pl.ds((d * pieces + k) * orr, orr)], ofull.at[o_rows_of(me, d, k)],
                      gos.at[d, 0, k], gor.at[d, 0, k], dp=hop[d])

    for c in strips:
        c.wait()
    for k in range(pieces):
        for d in range(2):
            first_q(d, k).start()

    for k in range(pieces):
        for d in range(2):
            @pl.when(own_out)
            def _():
                first_o(d, k).start()

    def origin(d, s):
        return ring_index((pos + n - s) % n if d == 0 else (pos + s) % n, n)

    def q_in(d, s, k):
        ref = q_at(origin(d, s), d, k)
        return remote(ref, ref, gqs.at[d, s - 1, k], gqr.at[d, s - 1, k], dp=hop[d])

    def q_on(d, s, k):
        ref = q_at(origin(d, s), d, k)
        return remote(ref, ref, gqs.at[d, s, k], gqr.at[d, s, k], dp=hop[d])

    def o_in(d, s, k):
        ref = ofull.at[o_rows_of(origin(d, s), d, k)]
        return remote(ref, ref, gos.at[d, s - 1, k], gor.at[d, s - 1, k], dp=hop[d])

    def o_on(d, s, k):
        ref = ofull.at[o_rows_of(origin(d, s), d, k)]
        return remote(ref, ref, gos.at[d, s, k], gor.at[d, s, k], dp=hop[d])

    def q_forward(s, last):
        for k in range(pieces):
            for d in range(2):
                q_in(d, s, k).wait_recv()
                if not last:
                    q_on(d, s, k).start()

    def o_forward(s, last):
        for k in range(pieces):
            for d in range(2):
                @pl.when(origin(d, s) // per == r)
                def _():
                    o_in(d, s, k).wait_recv()
                    if not last:
                        o_on(d, s, k).start()

    def project(s):
        for d in range(2):
            at = rows_at(origin(d, s) * q_rows + d * side, side)
            acc[...] += dg(norm_t[at], qfull[at], 0, 0)

    @pl.when(own_out)
    def _():
        ofull[rows_at((me % per) * o_rows, o_rows)] = ow[...]

    tfull[rows_at(r * rows, rows)] = tok[...]
    cfull[rows_at(r * rows, rows)] = cot[...]
    for j in range(1, count):
        for c in token_copies(j, (r + count - j) % count):
            c.wait_recv()
    for v in range(count):
        wide = tfull[pl.ds(v * rows, rows)].astype(F32)
        norm_t[:, pl.ds(v * rows, rows)] = (
            (wide * inverse_rms(wide) * gain[...]).astype(BF).T
        )
    acc[...] = jnp.zeros_like(acc)
    project(0)
    lag = min(2, n - 2)

    @pl.loop(1, n - 1)
    def _(s):
        q_forward(s, False)

        @pl.when(s > lag)
        def _():
            o_forward(s - lag, False)

        project(s)

    q_forward(n - 1, True)
    late = list(range(n - 1 - lag, n))
    o_forward(late[0], late[0] == n - 1)
    project(n - 1)
    proj[...] = acc[...].astype(BF)
    late = late[1:]

    for h in range(heads):
        @pl.when(section == 0)
        def _():
            query = jnp.concatenate(
                [proj[pl.ds(v * rows + half, half), head(h, 0)] for v in range(count)], 0
            )
            prob = softmax(query, proj[:, head(h, 1)])
            enc_prob[pl.ds(h * lats, lats)] = prob
            mixed[pl.ds(0, lats), pl.ds(h * HD, HD)] = dg(
                prob.astype(BF), proj[:, head(h, 2)], 1, 0
            ).astype(BF)

        if late:
            s = late.pop(0)
            o_forward(s, s == n - 1)
    for s in late:
        o_forward(s, s == n - 1)


    def partial(j):
        return remote(part.at[rows_at((r + j) % count * half, half)], got.at[j - 1],
                      psend.at[j - 1], precv.at[j - 1], render=(r + j) % count)

    def summed():
        for j in range(1, count):
            partial(j).start()
        total = part[mine].astype(F32)
        for j in range(1, count):
            partial(j).wait_recv()
            total = total + got[j - 1].astype(F32)
        return total

    def across(dst):
        return remote(own, dst.at[mine], xsend, xrecv, section=1 - section)

    def arrive(dst):
        across(dst).wait_recv()

        def forward(j, sender):
            ref = dst.at[rows_at(sender * half, half)]
            return remote(ref, ref, fsend.at[j - 1], frecv.at[j - 1], render=(r + j) % count)

        for j in range(1, count):
            forward(j, r).start()
        for j in range(1, count):
            forward(j, r).wait_send()
            forward(j, (r + count - j) % count).wait_recv()

    @pl.when(section == 0)
    def _():
        gain_lat[...] = jnp.zeros_like(gain_lat)
        part[...] = dg(mixed[pl.ds(0, lats)], ofull[...], 1, 0).astype(BF)
        own[...] = (tok[pl.ds(half, half)].astype(F32) + summed()).astype(BF)
        across(zfull).start()
        arrive(dz)
        opart[...] = dg(mixed[pl.ds(0, lats)], dz[...], 0, 0).astype(BF)

    @pl.when(section == 1)
    def _():
        gmix[...] = dg(cfull[...], ofull[...], 1, 1).astype(BF)
        arrive(zfull)
        wide = zfull[...].astype(F32)
        lat_norm[...] = (wide * inverse_rms(wide) * gain[...]).astype(BF)
        for h in range(heads):
            both = pl.ds(h * 2 * HD, 2 * HD)
            lat_kv[:, both] = dg(lat_norm[...], qfull[:, pair(h)], 1, 0).astype(BF)
        total = None
        for h in range(heads):
            lat_key = lat_kv[:, pl.ds(h * 2 * HD, HD)]
            lat_value = lat_kv[:, pl.ds(h * 2 * HD + HD, HD)]
            key_sum = jnp.zeros((lats, HD), F32)
            value_sum = jnp.zeros((lats, HD), F32)
            for v in range(count):
                at = pl.ds(v * rows, rows)
                query = proj[at, head(h, 0)]
                keys = jnp.concatenate([lat_key, proj[at, head(h, 1)]], 0)
                values = jnp.concatenate([lat_value, proj[at, head(h, 2)]], 0)
                prob = softmax(query, keys)
                rounded = prob.astype(BF)
                mixed[at, pl.ds(h * HD, HD)] = dg(rounded, values, 1, 0).astype(BF)
                upstream = gmix[at, pl.ds(h * HD, HD)]
                score = score_grad(prob, upstream, values)
                grads[at, head(h, 0)] = dg(score, keys, 1, 0).astype(BF)
                grad_key = dg(score, query, 0, 0)
                grad_value = dg(rounded, upstream, 0, 0)
                grads[at, head(h, 1)] = grad_key[lats:].astype(BF)
                grads[at, head(h, 2)] = grad_value[lats:].astype(BF)
                key_sum = key_sum + grad_key[:lats]
                value_sum = value_sum + grad_value[:lats]
            lat_grad[:, pl.ds(h * 2 * HD, HD)] = key_sum.astype(BF)
            lat_grad[:, pl.ds(h * 2 * HD + HD, HD)] = value_sum.astype(BF)
        total = dg(lat_grad[:, pl.ds(0, 2 * HD)], qfull[:, pair(0)], 1, 1)
        for h in range(1, heads):
            total = total + dg(lat_grad[:, pl.ds(h * 2 * HD, 2 * HD)], qfull[:, pair(h)], 1, 1)
        part[...] = total.astype(BF)
        grad = summed().astype(BF).astype(F32)
        back, gain_term = norm_back(zfull[mine].astype(F32), gain[...], grad)
        own[...] = back.astype(BF)
        gain_lat[...] = gain_term
        across(dz).start()
        opart[...] = dg(mixed[...], cfull[...], 0, 0).astype(BF)
        lat_t[...] = lat_norm[...].T


    def shard_at(d, s):
        return ring_index((pos + 2 * n - 1 - s) % n if d == 0 else (pos + 1 + s) % n, n)

    def q_copy(src, d, s, h):
        return remote(src, qbuf.at[d, s, h], qsend.at[d, s, h], qrecv.at[d, s, h], dp=hop[d])

    def o_copy(src, d, s, k):
        return remote(src, obuf.at[d, s, k], osend.at[d, s, k], orecv.at[d, s, k], dp=hop[d])

    def o_first(d, k):
        return o_copy(opart.at[o_rows_of(shard_at(d, 0), d, k)], d, 0, k)

    for k in range(pieces):
        for d in range(2):
            @pl.when(shard_at(d, 0) // per == r)
            def _():
                o_first(d, k).start()

    def own_term(shard, d, h):
        at = rows_at(shard * q_rows + d * side, side)
        qpart[d, h] = dg(norm_t[at], grads[:, pl.ds(h * wide_head, wide_head)], 1, 0)

        @pl.when(section == 1)
        def _():
            lat = dg(lat_t[at], lat_grad[:, pl.ds(h * 2 * HD, 2 * HD)], 1, 0)
            qpart[d, h, :, pl.ds(HD, 2 * HD)] += lat

    @pl.when(section == 0)
    def _():
        gmix[pl.ds(0, lats)] = dg(dz[...], ofull[...], 1, 1).astype(BF)

    for h in range(heads):
        @pl.when(section == 0)
        def _():
            prob = enc_prob[pl.ds(h * lats, lats)]
            upstream = gmix[pl.ds(0, lats), pl.ds(h * HD, HD)]
            query = jnp.concatenate(
                [proj[pl.ds(v * rows + half, half), head(h, 0)] for v in range(count)], 0
            )
            score = score_grad(prob, upstream, proj[:, head(h, 2)])
            grad_query = dg(score, proj[:, head(h, 1)], 1, 0).astype(BF)
            for v in range(count):
                grads[pl.ds(v * rows, half), head(h, 0)] = jnp.zeros((half, HD), BF)
                grads[pl.ds(v * rows + half, half), head(h, 0)] = (
                    grad_query[v * half : (v + 1) * half]
                )
            grads[:, head(h, 1)] = dg(score, query, 0, 0).astype(BF)
            grads[:, head(h, 2)] = dg(prob.astype(BF), upstream, 0, 0).astype(BF)

        for d in range(2):
            own_term(shard_at(d, 0), d, h)
            qbuf[d, n - 1, h] = qpart[d, h].astype(BF)
            q_copy(qbuf.at[d, n - 1, h], d, 0, h).start()

    dpart[...] = dg(grads[...], qfull[...], 1, 1).astype(BF)

    def block(j):
        peer = (r + j) % count
        return remote(dpart.at[rows_at(peer * rows, rows)], dbuf.at[j - 1],
                      dsend.at[j - 1], drecv.at[j - 1], render=peer)

    for j in range(1, count):
        block(j).start()
    total = dpart[rows_at(r * rows, rows)].astype(F32)
    for j in range(1, count):
        block(j).wait_recv()
        total = total + dbuf[j - 1].astype(F32)
    back, gain_term = norm_back(tok[...].astype(F32), gain[...], total.astype(BF).astype(F32))
    own_gain[...] = gain_lat[...] + gain_term

    @pl.when(section == 0)
    def _():
        tout[pl.ds(0, half)] = back[:half].astype(BF)
        tout[pl.ds(half, half)] = (back[half:] + dz[mine].astype(F32)).astype(BF)

    @pl.when(section == 1)
    def _():
        tout[...] = (back + cot[...].astype(F32)).astype(BF)

    def gain_copy(j, sender):
        other = (flat + j) % everyone
        return remote(own_gain, gbuf.at[sender], gsend.at[j], grecv.at[j],
                      dp=other // count, render=other % count)

    @pl.loop(1, everyone)
    def _(j):
        gain_copy(j, flat).start()

    @pl.loop(1, n - 1)
    def _(s):
        for h in range(heads):
            for d in range(2):
                own_term(shard_at(d, s), d, h)
        for h in range(heads):
            for d in range(2):
                held = qbuf.at[d, s - 1, h]
                q_copy(held, d, s - 1, h).wait_recv()
                held[...] = (held[...].astype(F32) + qpart[d, h]).astype(BF)
                q_copy(held, d, s, h).start()
        for k in range(pieces):
            for d in range(2):
                shard = shard_at(d, s)

                @pl.when(shard // per == r)
                def _():
                    held = obuf.at[d, s - 1, k]
                    o_copy(held, d, s - 1, k).wait_recv()
                    held[...] = (
                        held[...].astype(F32) + opart[o_rows_of(shard, d, k)].astype(F32)
                    ).astype(BF)
                    o_copy(held, d, s, k).start()

    def q_final(j, d, h, sender):
        ref = qout.at[sender, pl.ds(d * side, side), pl.ds(h * wide_head, wide_head)]
        return remote(ref, ref, esend.at[j - 1, d, h], erecv.at[j - 1, d, h],
                      render=(r + j) % count)

    def o_final(j, d, k):
        ref = oout.at[pl.ds((d * pieces + k) * orr, orr)]
        return remote(ref, ref, hsend.at[j - 1, d, k], hrecv.at[d, k], render=(r + j) % count)

    for h in range(heads):
        for d in range(2):
            own_term(me, d, h)

    gbuf[flat] = own_gain[...]

    @pl.loop(1, everyone)
    def _(j):
        gain_copy(j, (flat + everyone - j) % everyone).wait_recv()
        gain_copy(j, flat).wait_send()

    gout[...] = jnp.sum(gbuf[...], axis=0)

    for h in range(heads):
        for d in range(2):
            held = qbuf.at[d, n - 2, h]
            q_copy(held, d, n - 2, h).wait_recv()
            qout[r, pl.ds(d * side, side), pl.ds(h * wide_head, wide_head)] = (
                held[...].astype(F32) + qpart[d, h]
            ).astype(BF)
            for j in range(1, count):
                q_final(j, d, h, r).start()

    for k in range(pieces):
        for d in range(2):
            @pl.when(own_out)
            def _():
                held = obuf.at[d, n - 2, k]
                o_copy(held, d, n - 2, k).wait_recv()
                oout[pl.ds((d * pieces + k) * orr, orr)] = (
                    held[...].astype(F32) + opart[o_rows_of(me, d, k)].astype(F32)
                ).astype(BF)
                for j in range(1, count):
                    o_final(j, d, k).start()


    @pl.loop(0, n - 1)
    def _(s):
        for d in range(2):
            for h in range(heads):
                q_copy(qbuf.at[d, s, h], d, s, h).wait_send()
            for k in range(pieces):
                q_on(d, s, k).wait_send()

                @pl.when(origin(d, s) // per == r)
                def _():
                    o_on(d, s, k).wait_send()

                @pl.when(shard_at(d, s) // per == r)
                def _():
                    o_copy(obuf.at[d, s, k], d, s, k).wait_send()

    across(dz).wait_send()
    for j in range(1, count):
        for c in token_copies(j, r):
            c.wait_send()
        partial(j).wait_send()
        block(j).wait_send()
        for d in range(2):
            for h in range(heads):
                q_final(j, d, h, r).wait_send()
                q_final(j, d, h, (r + count - j) % count).wait_recv()
            for k in range(pieces):
                @pl.when(own_out)
                def _():
                    o_final(j, d, k).wait_send()

    @pl.when(jnp.logical_not(own_out))
    def _():
        for k in range(pieces):
            for d in range(2):
                o_final(1, d, k).wait_recv()


def whole_step(w, ow, tok, cot, gain):
    n, count = dims()
    q_rows, wide = w.shape[0], w.shape[1] // count
    o_rows, depth = ow.shape
    width = wide // 3
    heads = width // HD
    pieces = pieces_of(o_rows)
    orr = o_rows // (2 * pieces)
    rows = tok.shape[0]
    half = rows // 2
    lats = half * count
    scene = rows * count
    everyone = n * count
    sem = lambda *shape: pltpu.SemaphoreType.DMA(shape)
    one = pltpu.SemaphoreType.DMA
    mem = lambda *shape, t=BF: pltpu.VMEM(shape, t)
    ring = (2, n - 1, pieces)
    turn = (2, n - 1, heads)
    return call(
        functools.partial(step_kernel, n, count, width), 0,
        (jax.ShapeDtypeStruct((count, q_rows, wide), BF),
         jax.ShapeDtypeStruct((o_rows, depth), BF),
         jax.ShapeDtypeStruct(tok.shape, BF),
         jax.ShapeDtypeStruct(gain.shape, F32)),
        [ANY] + [VMEM] * 4, (VMEM,) * 4,
        [mem(depth, wide), mem(width, depth), mem(scene, depth), mem(scene, depth),
         mem(depth, scene), mem(scene, wide, t=F32), mem(scene, wide),
         mem(heads * lats, scene, t=F32), mem(scene, width), mem(scene, width),
         mem(lats, depth), mem(depth, lats), mem(lats, 2 * width), mem(lats, 2 * width),
         mem(scene, wide), mem(lats, depth), mem(lats, depth), mem(lats, depth),
         mem(half, depth), mem(count - 1, half, depth), mem(1, depth, t=F32),
         mem(2, heads, q_rows // 2, 3 * HD, t=F32), mem(width, depth), mem(scene, depth),
         mem(2, n, heads, q_rows // 2, 3 * HD), mem(*ring, orr, depth),
         mem(count - 1, rows, depth), mem(everyone, 1, depth, t=F32), mem(1, depth, t=F32), sem(heads, 3),
         sem(*ring), sem(*ring), sem(*ring), sem(*ring),
         sem(2, count - 1), sem(2, count - 1), sem(count - 1), sem(count - 1),
         one, one, sem(count - 1), sem(count - 1),
         sem(*turn), sem(*turn), sem(*ring), sem(*ring),
         sem(count - 1), sem(count - 1), sem(everyone), sem(everyone),
         sem(count - 1, 2, heads), sem(count - 1, 2, heads),
         sem(count - 1, 2, pieces), sem(2, pieces)],
        60, (w, ow, tok, cot, gain),
    )


def widen_kernel(q_ref, o_ref, qout, oout):
    count, _, wide = q_ref.shape
    width = wide // 3
    for c in range(count):
        for strip in range(3):
            for h in range(width // HD):
                qout[0, :, pl.ds((strip * count + c) * width + h * HD, HD)] = (
                    q_ref[c, :, pl.ds((3 * h + strip) * HD, HD)].astype(F32)
                )
    oout[0] = o_ref[...].astype(F32)


def widen(qsum, osum):
    count, q_rows, wide = qsum.shape
    o_rows, depth = osum.shape
    steps = 4
    qb, ob = q_rows // steps, o_rows // steps
    return pl.pallas_call(
        widen_kernel,
        grid=(steps,),
        out_shape=(jax.ShapeDtypeStruct((1, q_rows, count * wide), F32),
                   jax.ShapeDtypeStruct((1, o_rows, depth), F32)),
        in_specs=[pl.BlockSpec((count, qb, wide), lambda i: (0, i, 0)),
                  pl.BlockSpec((ob, depth), lambda i: (i, 0))],
        out_specs=(pl.BlockSpec((1, qb, count * wide), lambda i: (0, i, 0)),
                   pl.BlockSpec((1, ob, depth), lambda i: (0, i, 0))),
    )(qsum, osum)


def shards(section_tokens, w_qkv, w_out, gains, cotangent):
    qsum, osum, token_grad, gain_grad = whole_step(
        w_qkv[0], w_out[0], section_tokens[0, 0], cotangent[0], gains
    )
    qkv_grad, out_grad = widen(qsum, osum)
    return token_grad[None, None], qkv_grad, out_grad, gain_grad


def solution(mesh):
    in_specs = (
        P("section", "dp", "render", None),
        P("section", "dp", None),
        P("section", "dp", None),
        P("section", None),
        P("dp", "render", None),
    )
    out_specs = (
        P("section", "dp", "render", None),
        P("section", "dp", None),
        P("section", "dp", None),
        P("section", None),
    )
    return jax.shard_map(shards, mesh=mesh, in_specs=in_specs, out_specs=out_specs, check_vma=False)
```
